512 devices in a mesh: space: 64 (over z, x), radial: 8 (over y, core).
Axes of the slice: x: 4, y: 4, z: 16, core: 2. Of those that a mesh axis runs over, the one named last changes fastest.
Arguments:
- snapshots: float32 [32, 5, 1024, 1024], P(None, None, 'space', 'radial'), as said below
Outputs:
- modes: float32 [32, 5, 1024, 1024], P(None, None, 'space', 'radial')
- divergence: float32 [32, 5, 1024, 1024], P(None, None, 'space', 'radial')
- reduced: float32 [32, 32], replicated
Inputs may be any that keep to these rules, and one draw needn't show every extreme that they name: `snapshots`: density (variable 0) lies between 0.5 and 1.5; energy (variable 4) exceeds the kinetic energy by 1 or more.
All inputs are finite; a program needn't handle non-finite values.
Results may differ from the reference program's by a relative error of at most 0.0003.
Values sent between devices are 32-bit elements; how exact they have to be, the bound alone decides.
A program may use at most 64 MiB of HBM per device.

```python
import jax
import jax.numpy as jnp
from jax import lax

S = 32
NX = 1024
NR = 1024


def draw_snapshots(key, part):
    keys = jax.random.split(key, 3)
    rho = jax.random.uniform(keys[0], (S, NX, NR), jnp.float32, 0.5, 1.5)
    moment = 0.6 * jax.random.normal(keys[1], (3, S, NX, NR), jnp.float32)
    base = jax.random.uniform(keys[2], (S, NX, NR), jnp.float32, 1.0, 2.5)
    energy = base + 0.5 * jnp.sum(moment * moment, axis=0) / rho
    return jnp.stack([rho, moment[0], moment[1], moment[2], energy], axis=1)


def setup_inputs(seed: int = 0) -> dict:
    splits = jax.random.split(jax.random.key(seed), 2)
    return {
        "snapshots": draw_snapshots(jax.random.fold_in(splits[1], 71), 0),
    }


def flux_pair(snap):
    rho = snap[0]
    mom_a = snap[1]
    mom_b = snap[2]
    mom_c = snap[3]
    energy = snap[4]
    speed_a = mom_a / rho
    speed_b = mom_b / rho
    press = 0.4 * (energy - 0.5 * (mom_a * speed_a + mom_b * speed_b + mom_c * mom_c / rho))
    axial = jnp.stack([mom_a, mom_a * speed_a + press, mom_b * speed_a, mom_c * speed_a, (energy + press) * speed_a], 0)
    radial = jnp.stack([mom_b, mom_a * speed_b, mom_b * speed_b + press, mom_c * speed_b, (energy + press) * speed_b], 0)
    return (axial, radial)

def central(padded, dim, count):
    coeffs = (0.75, -0.15, 1.0 / 60.0)
    total = jnp.zeros_like(lax.slice_in_dim(padded, 3, 3 + count, axis=dim))
    for step in range(3):
        ahead = lax.slice_in_dim(padded, 3 + step + 1, 3 + step + 1 + count, axis=dim)
        behind = lax.slice_in_dim(padded, 3 - step - 1, 3 - step - 1 + count, axis=dim)
        total = total + coeffs[step] * (ahead - behind)
    return total

def one_snapshot(snap):
    axial, radial = flux_pair(snap)
    pad_a = jnp.pad(axial, ((0, 0), (3, 3), (0, 0)))
    pad_r = jnp.pad(radial, ((0, 0), (0, 0), (3, 3)))
    return -(central(pad_a, 1, axial.shape[1]) + central(pad_r, 2, axial.shape[2]))

def reference(snapshots):
    hp = lax.Precision.HIGHEST
    divergence = lax.map(one_snapshot, snapshots)
    count = snapshots.shape[1] * snapshots.shape[2] * snapshots.shape[3]
    gram = jnp.einsum('svxr,tvxr->st', snapshots, snapshots, precision=hp) / count
    factor = jnp.linalg.cholesky(gram)
    identity = jnp.eye(gram.shape[0], dtype=gram.dtype)
    lower = lax.linalg.triangular_solve(factor, identity, left_side=True, lower=True)
    modes = jnp.einsum('ks,svxr->kvxr', lower, snapshots, precision=hp)
    reduced = jnp.einsum('kvxr,jvxr->kj', modes, divergence, precision=hp) / jnp.sqrt(jnp.float32(count))
    return (modes, divergence, reduced)
```

```python
import functools
import itertools

import jax
import jax.numpy as jnp
from jax import lax
from jax.experimental import pallas as pl
from jax.experimental.pallas import tpu as pltpu
from jax.sharding import PartitionSpec as P

MESH = pl.DeviceIdType.MESH
F32 = jnp.float32
BF16 = jnp.bfloat16
HIGHEST = lax.Precision.HIGHEST
COEFFS = (0.75, -0.15, 1.0 / 60.0)
S, V, NI, NL = 32, 5, 16, 128
EDGE = (0, 1, 2, 13, 14, 15)
NT = (((1,), (1,)), ((), ()))
TN = (((0,), (0,)), ((), ()))


def split(a):
    high = a.astype(BF16)
    low = (a - high.astype(F32)).astype(BF16)
    return jnp.concatenate([high, low], axis=0)


def flux_state(q):
    rho, ma, mb, mc, energy = q
    inv = 1.0 / rho
    ua, ub, uc = ma * inv, mb * inv, mc * inv
    press = 0.4 * (energy - 0.5 * (ma * ua + mb * ub + mc * uc))
    return ua, ub, press


def flux_axial(q):
    _, ma, mb, mc, energy = q
    ua, _, press = flux_state(q)
    return (ma, ma * ua + press, mb * ua, mc * ua, (energy + press) * ua)


def flux_radial(q):
    _, ma, mb, mc, energy = q
    _, ub, press = flux_state(q)
    return (mb, ma * ub, mb * ub + press, mc * ub, (energy + press) * ub)


def flux_both(q):
    _, ma, mb, mc, energy = q
    ua, ub, press = flux_state(q)
    cross, total = mb * ua, energy + press
    axial = (ma, ma * ua + press, cross, mc * ua, total * ua)
    radial = (mb, cross, mb * ub + press, mc * ub, total * ub)
    return axial, radial


def pack(acc, tmp):
    tmp[...] = jnp.zeros_like(tmp)
    tmp[:, 0:64] = acc
    full = tmp[...]
    rows = full[0:32] + full[32:64]
    both = rows + pltpu.roll(rows, NL - 32, axis=1)
    lane = lax.broadcasted_iota(jnp.int32, (8, NL), 1)
    out = jnp.zeros((8, NL), F32)
    for r in range(4):
        part = both[8 * r : 8 * r + 8]
        if r:
            part = pltpu.roll(part, 32 * r, axis=1)
        out = jnp.where(lane // 32 == r, part, out)
    return out


def unpack(tile):
    return jnp.concatenate([tile] + [pltpu.roll(tile, NL - 32 * r, axis=1) for r in (1, 2, 3)], axis=0)


def inverse_factor(gram):
    row = lax.broadcasted_iota(jnp.int32, (S, NL), 0)
    lane = lax.broadcasted_iota(jnp.int32, (S, NL), 1)
    w = jnp.where(lane < S, gram, jnp.where(lane == row + S, 1.0, 0.0))
    for k in range(S - 1):
        pivot = w[k : k + 1, :]
        scale = w[:, k : k + 1] * (1.0 / w[k : k + 1, k : k + 1])
        w = w - jnp.where(row > k, scale, 0.0) * pivot
    diag = jnp.sum(jnp.where(lane == row, w, 0.0), axis=1, keepdims=True)
    low = pltpu.roll(w, NL - S, axis=1) * lax.rsqrt(diag)
    return jnp.where(lane < S, low, 0.0)


def ring(d, n):
    return min(d, n - d)


def main_kernel(dims, count, snap, modes, div, red, y, yp, fs, dt, mt, ed, ha, hr, tmp, sb, rc, rp, rz, load_sem, out_sem, send, recv):
    nz, nx, ny = dims
    nsp, nra = nz * nx, ny * 2
    sp, ra = lax.axis_index("space"), lax.axis_index("radial")
    z, x = sp // nx, sp % nx
    yy, c = ra // 2, ra % 2
    plane_offsets = sorted(
        [o for o in itertools.product(range(nx), range(ny)) if any(o)], key=lambda o: -ring(o[0], nx) - ring(o[1], ny)
    )
    deep_offsets = sorted(range(1, nz), key=lambda d: -ring(d, nz))

    def plane(o):
        return (z * nx + (x + o[0]) % nx, ((yy + o[1]) % ny) * 2 + c)

    def deep(d):
        return (((z + d) % nz) * nx + x, ra)

    core = (sp, yy * 2 + 1 - c)
    ahead_a, behind_a = ((sp + 1) % nsp, ra), ((sp + nsp - 1) % nsp, ra)
    ahead_r, behind_r = (sp, (ra + 1) % nra), (sp, (ra + nra - 1) % nra)

    barrier = pltpu.get_barrier_semaphore()
    peers = [deep(d) for d in deep_offsets] + [plane(o) for o in plane_offsets] + [core, ahead_a, behind_a, ahead_r, behind_r]
    for peer in peers:
        pl.semaphore_signal(barrier, inc=1, device_id=peer, device_id_type=MESH)
    for s in range(S):
        pltpu.make_async_copy(snap.at[s], y.at[:, :, s, :], load_sem).start()
    pltpu.make_async_copy(y, y, load_sem).wait()
    pl.semaphore_wait(barrier, len(peers))

    def remote(src, dst, k, peer):
        return pltpu.make_async_remote_copy(src, dst, send.at[k], recv.at[k], device_id=peer, device_id_type=MESH)

    halo = [remote(y.at[:, NI - 3 : NI], ha.at[0], 0, ahead_a), remote(y.at[:, 0:3], ha.at[1], 1, behind_a)]
    for h in halo:
        h.start()

    def start_core(k, tile):
        sb[3 * k] = tile
        remote(sb.at[3 * k], rc.at[k], 4 + 3 * k, core).start()

    def end_core(k):
        remote(sb.at[3 * k], rc.at[k], 4 + 3 * k, core).wait()
        return sb[3 * k] + rc[k]

    def start_many(k, stage, buf, mine, targets, tile):
        sb[3 * k + stage] = tile
        buf[k, mine] = tile
        for peer in targets:
            remote(sb.at[3 * k + stage], buf.at[k, mine], 4 + 3 * k + stage, peer).start()

    def end_many(k, stage, buf, n):
        landed = buf.at[k, 0 : n - 1]
        pltpu.make_async_copy(landed, landed, recv.at[4 + 3 * k + stage]).wait()
        pltpu.make_async_copy(landed, landed, send.at[4 + 3 * k + stage]).wait()
        parts = [buf[k, i] for i in range(n)]
        while len(parts) > 1:
            parts = [parts[i] + parts[i + 1] for i in range(0, len(parts), 2)]
        return parts[0]

    def start_plane(k, tile):
        start_many(k, 1, rp, x * ny + yy, [plane(o) for o in plane_offsets], tile)

    def end_plane(k):
        return end_many(k, 1, rp, nx * ny)

    def start_deep(k, tile):
        start_many(k, 2, rz, z, [deep(d) for d in deep_offsets], tile)

    def end_deep(k):
        return end_many(k, 2, rz, nz)

    def gram_step(v, acc):
        for i in range(NI):
            p = split(y[v, i])
            yp[v, i] = p
            acc = acc + lax.dot_general(p, p, NT, preferred_element_type=F32)
        return acc

    acc = lax.fori_loop(0, V, gram_step, jnp.zeros((2 * S, 2 * S), F32))
    start_core(0, pack(acc, tmp))

    row8 = lax.broadcasted_iota(jnp.int32, (8, NL), 0)
    lane8 = lax.broadcasted_iota(jnp.int32, (8, NL), 1)
    pick = jnp.where((row8 < 6) & (lane8 == jnp.where(row8 < 3, row8, row8 + NL - 6)), 1.0, 0.0)

    def edge_step(v, carry):
        for j in range(4):
            rows = y[v, 4 * j : 4 * j + 4].reshape(4 * S, NL)
            ed[v, j] = lax.dot_general(pick, rows, NT, preferred_element_type=F32, precision=HIGHEST)
        return carry

    lax.fori_loop(0, V, edge_step, 0)
    radial_halo = [remote(ed, hr.at[0], 2, ahead_r), remote(ed, hr.at[1], 3, behind_r)]
    for h in radial_halo:
        h.start()

    start_plane(0, end_core(0))

    lane1 = lax.broadcasted_iota(jnp.int32, (1, NL), 1)
    up = [jnp.where(lane1 + k < NL, cf, 0.0) for k, cf in zip((1, 2, 3), COEFFS)]
    down = [jnp.where(lane1 >= k, cf, 0.0) for k, cf in zip((1, 2, 3), COEFFS)]

    def flux_step(i, carry):
        axial, radial = flux_both([y[v, i] for v in range(V)])
        for v in range(V):
            fs[v, 3 + i] = axial[v]
            g = radial[v]
            total = jnp.zeros_like(g)
            for k in (1, 2, 3):
                total = total + (down[k - 1] * pltpu.roll(g, k, axis=1) - up[k - 1] * pltpu.roll(g, NL - k, axis=1))
            dt[v, i] = total
        return carry

    lax.fori_loop(0, NI, flux_step, 0)

    for h in radial_halo:
        h.wait()
    row = lax.broadcasted_iota(jnp.int32, (8, NL), 0)
    hs = []
    for v in range(V):
        cells = [jnp.where(row < 3, hr[1, v, j], hr[0, v, j]) for j in range(4)]
        if v == 0:
            cells = [jnp.where(row < 6, a, 1.0) for a in cells]
        hs.append(cells)
    valid = jnp.where(row < 3, jnp.where(ra < nra - 1, 1, 0), jnp.where((row < 6) & (ra > 0), 1, 0)) > 0
    step = jnp.where(row8 < 3, row8 + NL - lane8, lane8 + 6 - row8)
    weight = jnp.zeros((8, NL), F32)
    for k, cf in zip((1, 2, 3), COEFFS):
        weight = jnp.where(step == k, cf, weight)
    weight = jnp.where(row8 < 6, jnp.where(row8 < 3, -weight, weight), 0.0)
    edge_flux = [flux_radial([hs[v][j] for v in range(V)]) for j in range(4)]
    for v in range(V):
        for j in range(4):
            g = jnp.where(valid, edge_flux[j][v], 0.0)
            add = lax.dot_general(g, weight, TN, preferred_element_type=F32, precision=HIGHEST)
            dt[v, 4 * j : 4 * j + 4] = dt[v, 4 * j : 4 * j + 4] + add.reshape(4, S, NL)

    def axial_row(v, i):
        total = jnp.zeros((S, NL), F32)
        for k, cf in zip((1, 2, 3), COEFFS):
            total = total + cf * (fs[v, i + 3 - k] - fs[v, i + 3 + k])
        d = dt[v, i] + total
        dt[v, i] = d
        return lax.dot_general(yp[v, i], split(d), NT, preferred_element_type=F32)

    def inner_step(i, acc):
        for v in range(V):
            acc = acc + axial_row(v, i)
        return acc

    acc = lax.fori_loop(3, NI - 3, inner_step, jnp.zeros((2 * S, 2 * S), F32), unroll=2)

    start_deep(0, end_plane(0))

    for h in halo:
        h.wait()
    for side in range(2):
        keep = jnp.full((S, NL), jnp.where(sp > 0, 1, 0) if side == 0 else jnp.where(sp < nsp - 1, 1, 0)) > 0
        for j in range(3):
            axial = flux_axial([ha[side, v, j] for v in range(V)])
            for v in range(V):
                fs[v, j + (NI + 3) * side] = jnp.where(keep, axial[v], 0.0)
    for i in EDGE:
        acc = inner_step(i, acc)
    start_core(1, pack(acc, tmp))
    for s in range(S):
        pltpu.make_async_copy(dt.at[:, :, s, :], div.at[s], out_sem.at[0]).start()
    start_plane(1, end_core(1))
    gram = unpack(end_deep(0)) / count
    start_deep(1, end_plane(1))
    low = inverse_factor(gram)

    twice = low + pltpu.roll(low, S, axis=1)
    high = twice.astype(BF16)
    lhs = jnp.concatenate([high, (twice - high.astype(F32)).astype(BF16)], axis=0)[:, 0 : 2 * S]

    def mode_step(v, carry):
        for i in range(NI):
            out = jnp.dot(lhs, yp[v, i], preferred_element_type=F32)
            mt[v, i] = out[0:S] + out[S : 2 * S]
        return carry

    lax.fori_loop(0, V, mode_step, 0)
    for s in range(S):
        pltpu.make_async_copy(mt.at[:, :, s, :], modes.at[s], out_sem.at[1]).start()
    cross = unpack(end_deep(1))
    root = jnp.sqrt(jnp.full((S, S), count, F32))
    red[...] = jnp.dot(low[:, 0:S], cross[:, 0:S], preferred_element_type=F32, precision=HIGHEST) / root
    pltpu.make_async_copy(dt, dt, out_sem.at[0]).wait()
    pltpu.make_async_copy(mt, mt, out_sem.at[1]).wait()


def per_device(dims, snapshots):
    nz, nx, ny = dims
    count = float(V * NI * nz * nx * NL * ny * 2)
    vmem = pl.BlockSpec(memory_space=pltpu.VMEM)
    hbm = pl.BlockSpec(memory_space=pl.ANY)
    big = (S, V, NI, NL)
    dma = pltpu.SemaphoreType.DMA
    modes, div, red = pl.pallas_call(
        functools.partial(main_kernel, dims, count),
        out_shape=[pltpu.VMEM(big, F32), pltpu.VMEM(big, F32), pltpu.VMEM((S, S), F32)],
        in_specs=[hbm],
        out_specs=[vmem, vmem, vmem],
        scratch_shapes=[
            pltpu.VMEM((V, NI, S, NL), F32),
            pltpu.VMEM((V, NI, 2 * S, NL), BF16),
            pltpu.VMEM((V, NI + 6, S, NL), F32),
            pltpu.VMEM((V, NI, S, NL), F32),
            pltpu.VMEM((V, NI, S, NL), F32),
            pltpu.VMEM((V, 4, 8, NL), F32),
            pltpu.VMEM((2, V, 3, S, NL), F32),
            pltpu.VMEM((2, V, 4, 8, NL), F32),
            pltpu.VMEM((2 * S, NL), F32),
            pltpu.VMEM((6, 8, NL), F32),
            pltpu.VMEM((2, 8, NL), F32),
            pltpu.VMEM((2, nx * ny, 8, NL), F32),
            pltpu.VMEM((2, nz, 8, NL), F32),
            dma,
            dma((2,)),
            dma((10,)),
            dma((10,)),
        ],
        compiler_params=pltpu.CompilerParams(collective_id=0, has_side_effects=True),
    )(snapshots)
    return modes, div, red


def solution(mesh):
    space, radial = mesh.shape["space"], mesh.shape["radial"]
    nx = 4 if space > 4 else 2
    placed = P(None, None, "space", "radial")
    return jax.shard_map(
        functools.partial(per_device, (space // nx, nx, radial // 2)),
        mesh=mesh,
        in_specs=(placed,),
        out_specs=(placed, placed, P()),
        check_vma=False,
    )
```

```python
import functools
import itertools

import jax
import jax.numpy as jnp
from jax import lax
from jax.experimental import pallas as pl
from jax.experimental.pallas import tpu as pltpu
from jax.sharding import PartitionSpec as P

MESH = pl.DeviceIdType.MESH
F32 = jnp.float32
BF16 = jnp.bfloat16
HIGHEST = lax.Precision.HIGHEST
COEFFS = (0.75, -0.15, 1.0 / 60.0)
S, V, NI, NL = 32, 5, 16, 128
EDGE = (0, 1, 2, 13, 14, 15)
NT = (((1,), (1,)), ((), ()))
TN = (((0,), (0,)), ((), ()))


def split(a):
    high = a.astype(BF16)
    low = (a - high.astype(F32)).astype(BF16)
    return jnp.concatenate([high, low], axis=0)


def high_low(a):
    high = a.astype(BF16)
    return jnp.concatenate([high, (a - high.astype(F32)).astype(BF16)], axis=1)


def flux_state(q):
    rho, ma, mb, mc, energy = q
    inv = 1.0 / rho
    ua, ub, uc = ma * inv, mb * inv, mc * inv
    press = 0.4 * (energy - 0.5 * (ma * ua + mb * ub + mc * uc))
    return ua, ub, press


def flux_axial(q):
    _, ma, mb, mc, energy = q
    ua, _, press = flux_state(q)
    return (ma, ma * ua + press, mb * ua, mc * ua, (energy + press) * ua)


def flux_radial(q):
    _, ma, mb, mc, energy = q
    _, ub, press = flux_state(q)
    return (mb, ma * ub, mb * ub + press, mc * ub, (energy + press) * ub)


def flux_both(q):
    _, ma, mb, mc, energy = q
    ua, ub, press = flux_state(q)
    cross, total = mb * ua, energy + press
    axial = (ma, ma * ua + press, cross, mc * ua, total * ua)
    radial = (mb, cross, mb * ub + press, mc * ub, total * ub)
    return axial, radial


def pack(acc, tmp):
    tmp[...] = jnp.zeros_like(tmp)
    tmp[:, 0:64] = acc
    full = tmp[...]
    rows = full[0:32] + full[32:64]
    both = rows + pltpu.roll(rows, NL - 32, axis=1)
    lane = lax.broadcasted_iota(jnp.int32, (8, NL), 1)
    out = jnp.zeros((8, NL), F32)
    for r in range(4):
        part = both[8 * r : 8 * r + 8]
        if r:
            part = pltpu.roll(part, 32 * r, axis=1)
        out = jnp.where(lane // 32 == r, part, out)
    return out


def unpack(tile):
    return jnp.concatenate([tile] + [pltpu.roll(tile, NL - 32 * r, axis=1) for r in (1, 2, 3)], axis=0)


def inverse_factor(gram):
    row = lax.broadcasted_iota(jnp.int32, (S, NL), 0)
    lane = lax.broadcasted_iota(jnp.int32, (S, NL), 1)
    w = jnp.where(lane < S, gram, jnp.where(lane == row + S, 1.0, 0.0))
    for k in range(S - 1):
        pivot = w[k : k + 1, :]
        scale = w[:, k : k + 1] * (1.0 / w[k : k + 1, k : k + 1])
        w = w - jnp.where(row > k, scale, 0.0) * pivot
    diag = jnp.sum(jnp.where(lane == row, w, 0.0), axis=1, keepdims=True)
    low = pltpu.roll(w, NL - S, axis=1) * lax.rsqrt(diag)
    return jnp.where(lane < S, low, 0.0)


def ring(d, n):
    return min(d, n - d)


def offsets(n, steps):
    return sorted({d % n for k in steps for d in (k, -k)} - {0})


def main_kernel(dims, count, snap, modes, div, red, y, yp, fs, dt, mt, gs, gt, ed, ha, hr, tmp, sb, rc, rp, rz, known, load_sem, out_sem, send, recv):
    nz, nx, ny = dims
    nsp, nra = nz * nx, ny * 2
    sp, ra = lax.axis_index("space"), lax.axis_index("radial")
    z, x = sp // nx, sp % nx
    yy, c = ra // 2, ra % 2
    plane_offsets = sorted(
        [o for o in itertools.product(range(nx), range(ny)) if any(o)], key=lambda o: -ring(o[0], nx) - ring(o[1], ny)
    )
    deep_offsets = sorted(range(1, nz), key=lambda d: -ring(d, nz))

    def plane(o):
        return (z * nx + (x + o[0]) % nx, ((yy + o[1]) % ny) * 2 + c)

    def deep(d):
        return (((z + d) % nz) * nx + x, ra)

    core = (sp, yy * 2 + 1 - c)
    ahead_a, behind_a = ((sp + 1) % nsp, ra), ((sp + nsp - 1) % nsp, ra)
    ahead_r, behind_r = (sp, (ra + 1) % nra), (sp, (ra + nra - 1) % nra)

    barrier = pltpu.get_barrier_semaphore()
    line_x, line_y = [plane((d, 0)) for d in range(1, nx)], [plane((0, d)) for d in range(1, ny)]
    near_z, skip_z, far_z = [[deep(d) for d in offsets(nz, n)] for n in ((1, 2), (2,), (4,))]

    def signal(semaphore, targets):
        for peer in targets:
            pl.semaphore_signal(semaphore, inc=1, device_id=peer, device_id_type=MESH)
        return len(targets)

    near = signal(barrier, [ahead_a, behind_a, ahead_r, behind_r, core] + near_z + line_x + line_y)
    for s in range(S):
        pltpu.make_async_copy(snap.at[s], y.at[:, :, s, :], load_sem).start()
    pltpu.make_async_copy(y, y, load_sem).wait()
    pl.semaphore_wait(barrier, near)

    def remote(src, dst, k, peer):
        return pltpu.make_async_remote_copy(src, dst, send.at[k], recv.at[k], device_id=peer, device_id_type=MESH)

    halo = [remote(y.at[:, NI - 3 : NI], ha.at[0], 0, ahead_a), remote(y.at[:, 0:3], ha.at[1], 1, behind_a)]
    for h in halo:
        h.start()
    near = signal(known.at[0], line_x + skip_z)

    def start_core(k, tile):
        sb[3 * k] = tile
        remote(sb.at[3 * k], rc.at[k], 4 + 3 * k, core).start()

    def end_core(k):
        remote(sb.at[3 * k], rc.at[k], 4 + 3 * k, core).wait()
        return sb[3 * k] + rc[k]

    def start_many(k, stage, buf, mine, targets, tile):
        sb[3 * k + stage] = tile
        buf[k, mine] = tile
        for peer in targets:
            remote(sb.at[3 * k + stage], buf.at[k, mine], 4 + 3 * k + stage, peer).start()

    def end_many(k, stage, buf, n):
        landed = buf.at[k, 0 : n - 1]
        pltpu.make_async_copy(landed, landed, recv.at[4 + 3 * k + stage]).wait()
        pltpu.make_async_copy(landed, landed, send.at[4 + 3 * k + stage]).wait()
        parts = [buf[k, i] for i in range(n)]
        while len(parts) > 1:
            parts = [parts[i] + parts[i + 1] for i in range(0, len(parts), 2)]
        return parts[0]

    def start_plane(k, tile):
        start_many(k, 1, rp, x * ny + yy, [plane(o) for o in plane_offsets], tile)

    def end_plane(k):
        return end_many(k, 1, rp, nx * ny)

    def start_deep(k, tile):
        start_many(k, 2, rz, z, [deep(d) for d in deep_offsets], tile)

    def end_deep(k):
        return end_many(k, 2, rz, nz)

    row8 = lax.broadcasted_iota(jnp.int32, (8, NL), 0)
    lane8 = lax.broadcasted_iota(jnp.int32, (8, NL), 1)
    row16 = lax.broadcasted_iota(jnp.int32, (16, NL), 0)
    lane16 = lax.broadcasted_iota(jnp.int32, (16, NL), 1)
    pick = jnp.where((row16 < 6) & (lane16 == jnp.where(row16 < 3, row16, row16 + NL - 6)), 1.0, 0.0).astype(BF16)

    def gram_step(v, acc):
        for j in range(4):
            edge = []
            for i in range(4 * j, 4 * j + 4):
                p = split(y[v, i])
                yp[v, i] = p
                out = lax.dot_general(jnp.concatenate([p, pick], axis=0), p, NT, preferred_element_type=F32)
                acc = acc + out[0 : 2 * S]
                edge.append(out[2 * S : 2 * S + 8, 0:S] + out[2 * S : 2 * S + 8, S : 2 * S])
            ed[v, j] = jnp.concatenate(edge, axis=1)
        return acc

    acc = lax.fori_loop(0, V, gram_step, jnp.zeros((2 * S, 2 * S), F32))
    start_core(0, pack(acc, tmp))
    radial_halo = [remote(ed, hr.at[0], 2, ahead_r), remote(ed, hr.at[1], 3, behind_r)]
    for h in radial_halo:
        h.start()

    tile = end_core(0)
    pl.semaphore_wait(known.at[0], near)
    start_plane(0, tile)
    far = signal(known.at[1], far_z)

    def flux_step(i, carry):
        axial, radial = flux_both([y[v, i] for v in range(V)])
        for v in range(V):
            fs[v, 3 + i] = axial[v]
            high = radial[v].astype(BF16)
            gs[v, i, :, 0:NL] = high
            gs[v, i, :, NL : 2 * NL] = (radial[v] - high.astype(F32)).astype(BF16)
        return carry

    lax.fori_loop(0, NI, flux_step, 0)
    shift = lax.broadcasted_iota(jnp.int32, (NL, NL), 1) - lax.broadcasted_iota(jnp.int32, (NL, NL), 0)
    matrix = jnp.zeros((NL, NL), F32)
    for k, cf in zip((1, 2, 3), COEFFS):
        matrix = jnp.where(shift == k, cf, jnp.where(shift == -k, -cf, matrix))
    matrix = high_low(matrix)
    matrix = jnp.concatenate([matrix, matrix], axis=0)

    def radial_step(v, carry):
        out = jnp.dot(gs[v].reshape(NI * S, 2 * NL), matrix, preferred_element_type=F32)
        dt[v] = (out[:, 0:NL] + out[:, NL : 2 * NL]).reshape(NI, S, NL)
        return carry

    lax.fori_loop(0, V, radial_step, 0)

    for h in radial_halo:
        h.wait()
    step = jnp.where(row8 < 3, row8 + NL - lane8, lane8 + 6 - row8)
    weight = jnp.zeros((8, NL), F32)
    for k, cf in zip((1, 2, 3), COEFFS):
        weight = jnp.where(step == k, cf, weight)
    weight = jnp.where(row8 < 6, jnp.where(row8 < 3, -weight, weight), 0.0)
    weights = high_low(jnp.concatenate([weight] * 16, axis=0))
    group = (lax.broadcasted_iota(jnp.int32, (NL, 2 * NL), 0) // 8) % 8
    valid = jnp.where(row8 < 3, jnp.where(ra < nra - 1, 1, 0), jnp.where((row8 < 6) & (ra > 0), 1, 0)) > 0
    blank = jnp.zeros((24, NL), F32)
    for j in range(4):
        cells = [jnp.where(row8 < 3, hr[1, v, j], hr[0, v, j]) for v in range(V)]
        cells[0] = jnp.where(row8 < 6, cells[0], 1.0)
        rows = jnp.concatenate([jnp.where(valid, g, 0.0) for g in flux_radial(cells)], axis=0)
        high = rows.astype(BF16).astype(F32)
        rows = jnp.concatenate([high, blank, rows - high, blank], axis=0)
        gt[j] = rows.T.astype(BF16)
    for v in range(V):
        out = jnp.dot(gt[...].reshape(NI * S, NL), jnp.where(group == v, weights, 0.0).astype(BF16), preferred_element_type=F32)
        dt[v] = dt[v] + (out[:, 0:NL] + out[:, NL : 2 * NL]).reshape(NI, S, NL)

    def axial_row(v, i):
        total = jnp.zeros((S, NL), F32)
        for k, cf in zip((1, 2, 3), COEFFS):
            total = total + cf * (fs[v, i + 3 - k] - fs[v, i + 3 + k])
        d = dt[v, i] + total
        dt[v, i] = d
        return lax.dot_general(yp[v, i], split(d), NT, preferred_element_type=F32)

    def inner_step(i, acc):
        for v in range(V):
            acc = acc + axial_row(v, i)
        return acc

    acc = lax.fori_loop(3, NI - 3, inner_step, jnp.zeros((2 * S, 2 * S), F32), unroll=2)

    tile = end_plane(0)
    if far:
        pl.semaphore_wait(known.at[1], far)
    start_deep(0, tile)

    for h in halo:
        h.wait()
    for side in range(2):
        keep = jnp.full((S, NL), jnp.where(sp > 0, 1, 0) if side == 0 else jnp.where(sp < nsp - 1, 1, 0)) > 0
        for j in range(3):
            axial = flux_axial([ha[side, v, j] for v in range(V)])
            for v in range(V):
                fs[v, j + (NI + 3) * side] = jnp.where(keep, axial[v], 0.0)
    for i in EDGE:
        acc = inner_step(i, acc)
    start_core(1, pack(acc, tmp))
    for s in range(S):
        pltpu.make_async_copy(dt.at[:, :, s, :], div.at[s], out_sem.at[0]).start()
    start_plane(1, end_core(1))
    gram = unpack(end_deep(0)) / count
    start_deep(1, end_plane(1))
    low = inverse_factor(gram)

    twice = low + pltpu.roll(low, S, axis=1)
    high = twice.astype(BF16)
    lhs = jnp.concatenate([high, (twice - high.astype(F32)).astype(BF16)], axis=0)[:, 0 : 2 * S]

    def mode_step(v, carry):
        for i in range(NI):
            out = jnp.dot(lhs, yp[v, i], preferred_element_type=F32)
            mt[v, i] = out[0:S] + out[S : 2 * S]
        return carry

    lax.fori_loop(0, V, mode_step, 0)
    for s in range(S):
        pltpu.make_async_copy(mt.at[:, :, s, :], modes.at[s], out_sem.at[1]).start()
    cross = unpack(end_deep(1))
    root = jnp.sqrt(jnp.full((S, S), count, F32))
    red[...] = jnp.dot(low[:, 0:S], cross[:, 0:S], preferred_element_type=F32, precision=HIGHEST) / root
    pltpu.make_async_copy(dt, dt, out_sem.at[0]).wait()
    pltpu.make_async_copy(mt, mt, out_sem.at[1]).wait()


def write_kernel(modes, div, red, modes_out, div_out, red_out, sem):
    pairs = ((modes, modes_out), (div, div_out), (red, red_out))
    copies = [pltpu.make_async_copy(a, b, sem.at[i]) for i, (a, b) in enumerate(pairs)]
    for copy in copies:
        copy.start()
    for copy in copies:
        copy.wait()


def per_device(dims, snapshots):
    nz, nx, ny = dims
    count = float(V * NI * nz * nx * NL * ny * 2)
    vmem = pl.BlockSpec(memory_space=pltpu.VMEM)
    hbm = pl.BlockSpec(memory_space=pl.ANY)
    big = (S, V, NI, NL)
    dma = pltpu.SemaphoreType.DMA
    modes, div, red = pl.pallas_call(
        functools.partial(main_kernel, dims, count),
        out_shape=[pltpu.VMEM(big, F32), pltpu.VMEM(big, F32), pltpu.VMEM((S, S), F32)],
        in_specs=[hbm],
        out_specs=[vmem, vmem, vmem],
        scratch_shapes=[
            pltpu.VMEM((V, NI, S, NL), F32),
            pltpu.VMEM((V, NI, 2 * S, NL), BF16),
            pltpu.VMEM((V, NI + 6, S, NL), F32),
            pltpu.VMEM((V, NI, S, NL), F32),
            pltpu.VMEM((V, NI, S, NL), F32),
            pltpu.VMEM((V, NI, S, 2 * NL), BF16),
            pltpu.VMEM((4, NL, NL), BF16),
            pltpu.VMEM((V, 4, 8, NL), F32),
            pltpu.VMEM((2, V, 3, S, NL), F32),
            pltpu.VMEM((2, V, 4, 8, NL), F32),
            pltpu.VMEM((2 * S, NL), F32),
            pltpu.VMEM((6, 8, NL), F32),
            pltpu.VMEM((2, 8, NL), F32),
            pltpu.VMEM((2, nx * ny, 8, NL), F32),
            pltpu.VMEM((2, nz, 8, NL), F32),
            pltpu.SemaphoreType.REGULAR((2,)),
            dma,
            dma((2,)),
            dma((10,)),
            dma((10,)),
        ],
        compiler_params=pltpu.CompilerParams(collective_id=0, has_side_effects=True),
    )(snapshots)
    pinned = [pltpu.with_memory_space_constraint(a, pltpu.VMEM) for a in (modes, div, red)]
    modes, div, red = pl.pallas_call(
        write_kernel,
        out_shape=[jax.ShapeDtypeStruct(big, F32), jax.ShapeDtypeStruct(big, F32), jax.ShapeDtypeStruct((S, S), F32)],
        in_specs=[vmem, vmem, vmem],
        out_specs=[hbm, hbm, hbm],
        scratch_shapes=[dma((3,))],
    )(*pinned)
    return modes, div, red


def solution(mesh):
    space, radial = mesh.shape["space"], mesh.shape["radial"]
    nx = 4 if space > 4 else 2
    placed = P(None, None, "space", "radial")
    return jax.shard_map(
        functools.partial(per_device, (space // nx, nx, radial // 2)),
        mesh=mesh,
        in_specs=(placed,),
        out_specs=(placed, placed, P()),
        check_vma=False,
    )
```

```python
import functools

import jax
import jax.numpy as jnp
from jax import lax
from jax.experimental import pallas as pl
from jax.experimental.pallas import tpu as pltpu
from jax.sharding import PartitionSpec as P

MESH = pl.DeviceIdType.MESH
F32 = jnp.float32
BF16 = jnp.bfloat16
HIGHEST = lax.Precision.HIGHEST
COEFFS = (0.75, -0.15, 1.0 / 60.0)
S, V, NI, NL = 32, 5, 16, 128
EDGE = (0, 1, 2, 13, 14, 15)
NT = (((1,), (1,)), ((), ()))
TN = (((0,), (0,)), ((), ()))


def split(a):
    high = a.astype(BF16)
    low = (a - high.astype(F32)).astype(BF16)
    return jnp.concatenate([high, low], axis=0)


def high_low(a):
    high = a.astype(BF16)
    return jnp.concatenate([high, (a - high.astype(F32)).astype(BF16)], axis=1)


def flux_state(q):
    rho, ma, mb, mc, energy = q
    inv = 1.0 / rho
    ua, ub, uc = ma * inv, mb * inv, mc * inv
    press = 0.4 * (energy - 0.5 * (ma * ua + mb * ub + mc * uc))
    return ua, ub, press


def flux_axial(q):
    _, ma, mb, mc, energy = q
    ua, _, press = flux_state(q)
    return (ma, ma * ua + press, mb * ua, mc * ua, (energy + press) * ua)


def flux_radial(q):
    _, ma, mb, mc, energy = q
    _, ub, press = flux_state(q)
    return (mb, ma * ub, mb * ub + press, mc * ub, (energy + press) * ub)


def flux_both(q):
    _, ma, mb, mc, energy = q
    ua, ub, press = flux_state(q)
    cross, total = mb * ua, energy + press
    axial = (ma, ma * ua + press, cross, mc * ua, total * ua)
    radial = (mb, cross, mb * ub + press, mc * ub, total * ub)
    return axial, radial


def pack(acc, tmp):
    tmp[...] = jnp.zeros_like(tmp)
    tmp[:, 0:64] = acc
    full = tmp[...]
    rows = full[0:32] + full[32:64]
    both = rows + pltpu.roll(rows, NL - 32, axis=1)
    lane = lax.broadcasted_iota(jnp.int32, (8, NL), 1)
    out = jnp.zeros((8, NL), F32)
    for r in range(4):
        part = both[8 * r : 8 * r + 8]
        if r:
            part = pltpu.roll(part, 32 * r, axis=1)
        out = jnp.where(lane // 32 == r, part, out)
    return out


def unpack(tile):
    return jnp.concatenate([tile] + [pltpu.roll(tile, NL - 32 * r, axis=1) for r in (1, 2, 3)], axis=0)


def inverse_factor(gram):
    row = lax.broadcasted_iota(jnp.int32, (S, NL), 0)
    lane = lax.broadcasted_iota(jnp.int32, (S, NL), 1)
    w = jnp.where(lane < S, gram, jnp.where(lane == row + S, 1.0, 0.0))
    for k in range(S - 1):
        pivot = w[k : k + 1, :]
        scale = w[:, k : k + 1] * (1.0 / w[k : k + 1, k : k + 1])
        w = w - jnp.where(row > k, scale, 0.0) * pivot
    diag = jnp.sum(jnp.where(lane == row, w, 0.0), axis=1, keepdims=True)
    low = pltpu.roll(w, NL - S, axis=1) * lax.rsqrt(diag)
    return jnp.where(lane < S, low, 0.0)


def offsets(n, steps):
    return sorted({d % n for k in steps for d in (k, -k)} - {0})


def main_kernel(dims, count, snap, modes, div, red, y, yp, fs, dt, mt, gs, gt, ed, ha, hr, tmp, sb, rc, rp, rz, known, load_sem, out_sem, send, recv):
    nz, nx, ny = dims
    nsp, nra = nz * nx, ny * 2
    sp, ra = lax.axis_index("space"), lax.axis_index("radial")
    z, x = sp // nx, sp % nx
    yy, c = ra // 2, ra % 2
    def plane(o):
        return (z * nx + (x + o[0]) % nx, ((yy + o[1]) % ny) * 2 + c)

    def deep(d):
        return (((z + d) % nz) * nx + x, ra)

    def nth_plane(n):
        half_x, half_y = nx // 2, ny // 2
        own = (nx - half_x) % nx * ny + (ny - half_y) % ny
        n = jnp.where(n >= own, n + 1, n)
        return plane((half_x + n // ny, half_y + n % ny))

    def nth_deep(n):
        return deep(nz // 2 + jnp.where(n % 2 == 1, nz - (n + 1) // 2, n // 2))

    core = (sp, yy * 2 + 1 - c)
    ahead_a, behind_a = ((sp + 1) % nsp, ra), ((sp + nsp - 1) % nsp, ra)
    ahead_r, behind_r = (sp, (ra + 1) % nra), (sp, (ra + nra - 1) % nra)

    barrier = pltpu.get_barrier_semaphore()
    line_x, line_y = [plane((d, 0)) for d in range(1, nx)], [plane((0, d)) for d in range(1, ny)]
    near_z, skip_z, far_z = [[deep(d) for d in offsets(nz, n)] for n in ((1, 2), (2,), (4,))]

    def signal(semaphore, targets):
        for peer in targets:
            pl.semaphore_signal(semaphore, inc=1, device_id=peer, device_id_type=MESH)
        return len(targets)

    near = signal(barrier, [ahead_a, behind_a, ahead_r, behind_r, core] + near_z + line_x + line_y)
    for s in range(S):
        pltpu.make_async_copy(snap.at[s], y.at[:, :, s, :], load_sem).start()
    pltpu.make_async_copy(y, y, load_sem).wait()
    pl.semaphore_wait(barrier, near)

    def remote(src, dst, k, peer):
        return pltpu.make_async_remote_copy(src, dst, send.at[k], recv.at[k], device_id=peer, device_id_type=MESH)

    halo = [remote(y.at[:, NI - 3 : NI], ha.at[0], 0, ahead_a), remote(y.at[:, 0:3], ha.at[1], 1, behind_a)]
    for h in halo:
        h.start()
    near = signal(known.at[0], line_x + skip_z)

    def start_core(k, tile):
        sb[3 * k] = tile
        remote(sb.at[3 * k], rc.at[k], 4 + 3 * k, core).start()

    def end_core(k):
        remote(sb.at[3 * k], rc.at[k], 4 + 3 * k, core).wait()
        return sb[3 * k] + rc[k]

    def start_many(k, stage, buf, mine, n, target, tile):
        sb[3 * k + stage] = tile
        buf[k, mine] = tile

        def send_one(i, carry):
            remote(sb.at[3 * k + stage], buf.at[k, mine], 4 + 3 * k + stage, target(i)).start()
            return carry

        lax.fori_loop(0, n - 1, send_one, 0)

    def end_many(k, stage, buf, n):
        landed = buf.at[k, 0 : n - 1]
        pltpu.make_async_copy(landed, landed, recv.at[4 + 3 * k + stage]).wait()
        pltpu.make_async_copy(landed, landed, send.at[4 + 3 * k + stage]).wait()
        parts = [buf[k, i] for i in range(n)]
        while len(parts) > 1:
            parts = [parts[i] + parts[i + 1] for i in range(0, len(parts), 2)]
        return parts[0]

    def start_plane(k, tile):
        start_many(k, 1, rp, x * ny + yy, nx * ny, nth_plane, tile)

    def end_plane(k):
        return end_many(k, 1, rp, nx * ny)

    def start_deep(k, tile):
        start_many(k, 2, rz, z, nz, nth_deep, tile)

    def end_deep(k):
        return end_many(k, 2, rz, nz)

    row8 = lax.broadcasted_iota(jnp.int32, (8, NL), 0)
    lane8 = lax.broadcasted_iota(jnp.int32, (8, NL), 1)
    row16 = lax.broadcasted_iota(jnp.int32, (16, NL), 0)
    lane16 = lax.broadcasted_iota(jnp.int32, (16, NL), 1)
    pick = jnp.where((row16 < 6) & (lane16 == jnp.where(row16 < 3, row16, row16 + NL - 6)), 1.0, 0.0).astype(BF16)

    def gram_step(v, acc):
        for j in range(4):
            edge = []
            for i in range(4 * j, 4 * j + 4):
                p = split(y[v, i])
                yp[v, i] = p
                out = lax.dot_general(jnp.concatenate([p, pick], axis=0), p, NT, preferred_element_type=F32)
                acc = acc + out[0 : 2 * S]
                edge.append(out[2 * S : 2 * S + 8, 0:S] + out[2 * S : 2 * S + 8, S : 2 * S])
            ed[v, j] = jnp.concatenate(edge, axis=1)
        return acc

    acc = lax.fori_loop(0, V, gram_step, jnp.zeros((2 * S, 2 * S), F32))
    start_core(0, pack(acc, tmp))
    radial_halo = [remote(ed, hr.at[0], 2, ahead_r), remote(ed, hr.at[1], 3, behind_r)]
    for h in radial_halo:
        h.start()


    def flux_step(i, carry):
        axial, radial = flux_both([y[v, i] for v in range(V)])
        for v in range(V):
            fs[v, 3 + i] = axial[v]
            high = radial[v].astype(BF16)
            gs[v, i, :, 0:NL] = high
            gs[v, i, :, NL : 2 * NL] = (radial[v] - high.astype(F32)).astype(BF16)
        return carry

    lax.fori_loop(0, NI, flux_step, 0)
    tile = end_core(0)
    pl.semaphore_wait(known.at[0], near)
    start_plane(0, tile)
    far = signal(known.at[1], far_z)
    shift = lax.broadcasted_iota(jnp.int32, (NL, NL), 1) - lax.broadcasted_iota(jnp.int32, (NL, NL), 0)
    matrix = jnp.zeros((NL, NL), F32)
    for k, cf in zip((1, 2, 3), COEFFS):
        matrix = jnp.where(shift == k, cf, jnp.where(shift == -k, -cf, matrix))
    matrix = high_low(matrix)
    matrix = jnp.concatenate([matrix, matrix], axis=0)

    def radial_step(v, carry):
        out = jnp.dot(gs[v].reshape(NI * S, 2 * NL), matrix, preferred_element_type=F32)
        dt[v] = (out[:, 0:NL] + out[:, NL : 2 * NL]).reshape(NI, S, NL)
        return carry

    lax.fori_loop(0, V, radial_step, 0)

    for h in radial_halo:
        h.wait()
    step = jnp.where(row8 < 3, row8 + NL - lane8, lane8 + 6 - row8)
    weight = jnp.zeros((8, NL), F32)
    for k, cf in zip((1, 2, 3), COEFFS):
        weight = jnp.where(step == k, cf, weight)
    weight = jnp.where(row8 < 6, jnp.where(row8 < 3, -weight, weight), 0.0)
    weights = high_low(jnp.concatenate([weight] * 16, axis=0))
    group = (lax.broadcasted_iota(jnp.int32, (NL, 2 * NL), 0) // 8) % 8
    valid = jnp.where(row8 < 3, jnp.where(ra < nra - 1, 1, 0), jnp.where((row8 < 6) & (ra > 0), 1, 0)) > 0
    blank = jnp.zeros((24, NL), F32)
    for j in range(4):
        cells = [jnp.where(row8 < 3, hr[1, v, j], hr[0, v, j]) for v in range(V)]
        cells[0] = jnp.where(row8 < 6, cells[0], 1.0)
        rows = jnp.concatenate([jnp.where(valid, g, 0.0) for g in flux_radial(cells)], axis=0)
        high = rows.astype(BF16).astype(F32)
        rows = jnp.concatenate([high, blank, rows - high, blank], axis=0)
        gt[j] = rows.T.astype(BF16)
    for v in range(V):
        out = jnp.dot(gt[...].reshape(NI * S, NL), jnp.where(group == v, weights, 0.0).astype(BF16), preferred_element_type=F32)
        dt[v] = dt[v] + (out[:, 0:NL] + out[:, NL : 2 * NL]).reshape(NI, S, NL)

    def axial_row(v, i):
        total = jnp.zeros((S, NL), F32)
        for k, cf in zip((1, 2, 3), COEFFS):
            total = total + cf * (fs[v, i + 3 - k] - fs[v, i + 3 + k])
        d = dt[v, i] + total
        dt[v, i] = d
        return lax.dot_general(yp[v, i], split(d), NT, preferred_element_type=F32)

    def inner_step(i, acc):
        for v in range(V):
            acc = acc + axial_row(v, i)
        return acc

    acc = lax.fori_loop(3, NI - 3, inner_step, jnp.zeros((2 * S, 2 * S), F32), unroll=2)

    tile = end_plane(0)
    if far:
        pl.semaphore_wait(known.at[1], far)
    start_deep(0, tile)

    for h in halo:
        h.wait()
    for side in range(2):
        keep = jnp.full((S, NL), jnp.where(sp > 0, 1, 0) if side == 0 else jnp.where(sp < nsp - 1, 1, 0)) > 0
        for j in range(3):
            axial = flux_axial([ha[side, v, j] for v in range(V)])
            for v in range(V):
                fs[v, j + (NI + 3) * side] = jnp.where(keep, axial[v], 0.0)
    for i in EDGE:
        acc = inner_step(i, acc)
    start_core(1, pack(acc, tmp))
    start_plane(1, end_core(1))
    for s in range(S):
        pltpu.make_async_copy(dt.at[:, :, s, :], div.at[s], out_sem.at[0]).start()
    start_deep(1, end_plane(1))
    gram = unpack(end_deep(0)) / count
    low = inverse_factor(gram)

    twice = low + pltpu.roll(low, S, axis=1)
    high = twice.astype(BF16)
    lhs = jnp.concatenate([high, (twice - high.astype(F32)).astype(BF16)], axis=0)[:, 0 : 2 * S]

    def mode_step(v, carry):
        for i in range(NI):
            out = jnp.dot(lhs, yp[v, i], preferred_element_type=F32)
            mt[v, i] = out[0:S] + out[S : 2 * S]
        return carry

    lax.fori_loop(0, V, mode_step, 0)
    for s in range(S):
        pltpu.make_async_copy(mt.at[:, :, s, :], modes.at[s], out_sem.at[1]).start()
    cross = unpack(end_deep(1))
    root = jnp.sqrt(jnp.full((S, S), count, F32))
    red[...] = jnp.dot(low[:, 0:S], cross[:, 0:S], preferred_element_type=F32, precision=HIGHEST) / root
    pltpu.make_async_copy(dt, dt, out_sem.at[0]).wait()
    pltpu.make_async_copy(mt, mt, out_sem.at[1]).wait()


def write_kernel(modes, div, red, modes_out, div_out, red_out, sem):
    pairs = ((modes, modes_out), (div, div_out), (red, red_out))
    copies = [pltpu.make_async_copy(a, b, sem.at[i]) for i, (a, b) in enumerate(pairs)]
    for copy in copies:
        copy.start()
    for copy in copies:
        copy.wait()


def per_device(dims, snapshots):
    nz, nx, ny = dims
    count = float(V * NI * nz * nx * NL * ny * 2)
    vmem = pl.BlockSpec(memory_space=pltpu.VMEM)
    hbm = pl.BlockSpec(memory_space=pl.ANY)
    big = (S, V, NI, NL)
    dma = pltpu.SemaphoreType.DMA
    modes, div, red = pl.pallas_call(
        functools.partial(main_kernel, dims, count),
        out_shape=[pltpu.VMEM(big, F32), pltpu.VMEM(big, F32), pltpu.VMEM((S, S), F32)],
        in_specs=[hbm],
        out_specs=[vmem, vmem, vmem],
        scratch_shapes=[
            pltpu.VMEM((V, NI, S, NL), F32),
            pltpu.VMEM((V, NI, 2 * S, NL), BF16),
            pltpu.VMEM((V, NI + 6, S, NL), F32),
            pltpu.VMEM((V, NI, S, NL), F32),
            pltpu.VMEM((V, NI, S, NL), F32),
            pltpu.VMEM((V, NI, S, 2 * NL), BF16),
            pltpu.VMEM((4, NL, NL), BF16),
            pltpu.VMEM((V, 4, 8, NL), F32),
            pltpu.VMEM((2, V, 3, S, NL), F32),
            pltpu.VMEM((2, V, 4, 8, NL), F32),
            pltpu.VMEM((2 * S, NL), F32),
            pltpu.VMEM((6, 8, NL), F32),
            pltpu.VMEM((2, 8, NL), F32),
            pltpu.VMEM((2, nx * ny, 8, NL), F32),
            pltpu.VMEM((2, nz, 8, NL), F32),
            pltpu.SemaphoreType.REGULAR((2,)),
            dma,
            dma((2,)),
            dma((10,)),
            dma((10,)),
        ],
        compiler_params=pltpu.CompilerParams(collective_id=0, has_side_effects=True),
    )(snapshots)
    pinned = [pltpu.with_memory_space_constraint(a, pltpu.VMEM) for a in (modes, div, red)]
    modes, div, red = pl.pallas_call(
        write_kernel,
        out_shape=[jax.ShapeDtypeStruct(big, F32), jax.ShapeDtypeStruct(big, F32), jax.ShapeDtypeStruct((S, S), F32)],
        in_specs=[vmem, vmem, vmem],
        out_specs=[hbm, hbm, hbm],
        scratch_shapes=[dma((3,))],
    )(*pinned)
    return modes, div, red


def solution(mesh):
    space, radial = mesh.shape["space"], mesh.shape["radial"]
    nx = 4 if space > 4 else 2
    placed = P(None, None, "space", "radial")
    return jax.shard_map(
        functools.partial(per_device, (space // nx, nx, radial // 2)),
        mesh=mesh,
        in_specs=(placed,),
        out_specs=(placed, placed, P()),
        check_vma=False,
    )
```

```python
import functools

import jax
import jax.numpy as jnp
from jax import lax
from jax.experimental import pallas as pl
from jax.experimental.pallas import tpu as pltpu
from jax.sharding import PartitionSpec as P

MESH = pl.DeviceIdType.MESH
F32 = jnp.float32
BF16 = jnp.bfloat16
HIGHEST = lax.Precision.HIGHEST
COEFFS = (0.75, -0.15, 1.0 / 60.0)
S, V, NI, NL = 32, 5, 16, 128
NT = (((1,), (1,)), ((), ()))
TN = (((0,), (0,)), ((), ()))


def split(a):
    high = a.astype(BF16)
    low = (a - high.astype(F32)).astype(BF16)
    return jnp.concatenate([high, low], axis=0)


def high_low(a):
    high = a.astype(BF16)
    return jnp.concatenate([high, (a - high.astype(F32)).astype(BF16)], axis=1)


def flux_state(q):
    rho, ma, mb, mc, energy = q
    inv = 1.0 / rho
    ua, ub, uc = ma * inv, mb * inv, mc * inv
    press = 0.4 * (energy - 0.5 * (ma * ua + mb * ub + mc * uc))
    return ua, ub, press


def flux_axial(q):
    _, ma, mb, mc, energy = q
    ua, _, press = flux_state(q)
    return (ma, ma * ua + press, mb * ua, mc * ua, (energy + press) * ua)


def flux_radial(q):
    _, ma, mb, mc, energy = q
    _, ub, press = flux_state(q)
    return (mb, ma * ub, mb * ub + press, mc * ub, (energy + press) * ub)


def flux_both(q):
    _, ma, mb, mc, energy = q
    ua, ub, press = flux_state(q)
    cross, total = mb * ua, energy + press
    axial = (ma, ma * ua + press, cross, mc * ua, total * ua)
    radial = (mb, cross, mb * ub + press, mc * ub, total * ub)
    return axial, radial


def pack(acc, tmp):
    tmp[...] = jnp.zeros_like(tmp)
    tmp[:, 0:64] = acc
    full = tmp[...]
    rows = full[0:32] + full[32:64]
    both = rows + pltpu.roll(rows, NL - 32, axis=1)
    lane = lax.broadcasted_iota(jnp.int32, (8, NL), 1)
    out = jnp.zeros((8, NL), F32)
    for r in range(4):
        part = both[8 * r : 8 * r + 8]
        if r:
            part = pltpu.roll(part, 32 * r, axis=1)
        out = jnp.where(lane // 32 == r, part, out)
    return out


def unpack(tile):
    return jnp.concatenate([tile] + [pltpu.roll(tile, NL - 32 * r, axis=1) for r in (1, 2, 3)], axis=0)


def inverse_factor(gram):
    row = lax.broadcasted_iota(jnp.int32, (S, NL), 0)
    lane = lax.broadcasted_iota(jnp.int32, (S, NL), 1)
    w = jnp.where(lane < S, gram, jnp.where(lane == row + S, 1.0, 0.0))
    for k in range(S - 1):
        pivot = w[k : k + 1, :]
        scale = w[:, k : k + 1] * (1.0 / w[k : k + 1, k : k + 1])
        w = w - jnp.where(row > k, scale, 0.0) * pivot
    diag = jnp.sum(jnp.where(lane == row, w, 0.0), axis=1, keepdims=True)
    low = pltpu.roll(w, NL - S, axis=1) * lax.rsqrt(diag)
    return jnp.where(lane < S, low, 0.0)


def offsets(n, steps):
    return sorted({d % n for k in steps for d in (k, -k)} - {0})


def main_kernel(dims, count, snap, modes, div, red, y, yp, fs, fh, dt, mt, gs, gt, ed, ha, hr, tmp, sb, rc, rp, rz, known, load_sem, out_sem, send, recv):
    nz, nx, ny = dims
    nsp, nra = nz * nx, ny * 2
    sp, ra = lax.axis_index("space"), lax.axis_index("radial")
    z, x = sp // nx, sp % nx
    yy, c = ra // 2, ra % 2
    def plane(o):
        return (z * nx + (x + o[0]) % nx, ((yy + o[1]) % ny) * 2 + c)

    def deep(d):
        return (((z + d) % nz) * nx + x, ra)

    def nth_plane(n):
        half_x, half_y = nx // 2, ny // 2
        own = (nx - half_x) % nx * ny + (ny - half_y) % ny
        n = jnp.where(n >= own, n + 1, n)
        return plane((half_x + n // ny, half_y + n % ny))

    def nth_deep(n):
        return deep(nz // 2 + jnp.where(n % 2 == 1, nz - (n + 1) // 2, n // 2))

    core = (sp, yy * 2 + 1 - c)
    ahead_a, behind_a = ((sp + 1) % nsp, ra), ((sp + nsp - 1) % nsp, ra)
    ahead_r, behind_r = (sp, (ra + 1) % nra), (sp, (ra + nra - 1) % nra)

    barrier = pltpu.get_barrier_semaphore()
    line_x, line_y = [plane((d, 0)) for d in range(1, nx)], [plane((0, d)) for d in range(1, ny)]
    near_z, skip_z, far_z = [[deep(d) for d in offsets(nz, n)] for n in ((1, 2), (2,), (4,))]

    def signal(semaphore, targets):
        for peer in targets:
            pl.semaphore_signal(semaphore, inc=1, device_id=peer, device_id_type=MESH)
        return len(targets)

    near = signal(barrier, [ahead_a, behind_a, ahead_r, behind_r, core] + near_z + line_x + line_y)
    for s in range(S):
        pltpu.make_async_copy(snap.at[s], y.at[:, :, s, :], load_sem).start()
    pltpu.make_async_copy(y, y, load_sem).wait()
    pl.semaphore_wait(barrier, near)

    def remote(src, dst, k, peer):
        return pltpu.make_async_remote_copy(src, dst, send.at[k], recv.at[k], device_id=peer, device_id_type=MESH)

    first_halo = remote(y.at[:, pl.ds((1 - c) * (NI - 3), 3)], ha.at[c], 0, ((sp + nsp + 1 - 2 * c) % nsp, ra))
    other_halo = remote(y.at[:, pl.ds(c * (NI - 3), 3)], ha.at[1 - c], 1, ((sp + nsp - 1 + 2 * c) % nsp, ra))
    first_halo.start()
    near = signal(known.at[0], line_x + skip_z)

    def start_core(k, tile):
        sb[3 * k] = tile
        remote(sb.at[3 * k], rc.at[k], 4 + 3 * k, core).start()

    def end_core(k):
        remote(sb.at[3 * k], rc.at[k], 4 + 3 * k, core).wait()
        return sb[3 * k] + rc[k]

    def start_many(k, stage, buf, mine, n, target, tile):
        sb[3 * k + stage] = tile
        buf[k, mine] = tile

        def send_one(i, carry):
            remote(sb.at[3 * k + stage], buf.at[k, mine], 4 + 3 * k + stage, target(i)).start()
            return carry

        lax.fori_loop(0, n - 1, send_one, 0)

    def end_many(k, stage, buf, n):
        landed = buf.at[k, 0 : n - 1]
        pltpu.make_async_copy(landed, landed, recv.at[4 + 3 * k + stage]).wait()
        pltpu.make_async_copy(landed, landed, send.at[4 + 3 * k + stage]).wait()
        parts = [buf[k, i] for i in range(n)]
        while len(parts) > 1:
            parts = [parts[i] + parts[i + 1] for i in range(0, len(parts), 2)]
        return parts[0]

    def start_plane(k, tile):
        start_many(k, 1, rp, x * ny + yy, nx * ny, nth_plane, tile)

    def end_plane(k):
        return end_many(k, 1, rp, nx * ny)

    def start_deep(k, tile):
        start_many(k, 2, rz, z, nz, nth_deep, tile)

    def end_deep(k):
        return end_many(k, 2, rz, nz)

    row8 = lax.broadcasted_iota(jnp.int32, (8, NL), 0)
    lane8 = lax.broadcasted_iota(jnp.int32, (8, NL), 1)
    row16 = lax.broadcasted_iota(jnp.int32, (16, 2 * NL), 0)
    lane16 = lax.broadcasted_iota(jnp.int32, (16, 2 * NL), 1)
    cell = row16 % 8
    pick = (cell < 6) & (lane16 == row16 // 8 * NL + jnp.where(cell < 3, cell, cell + NL - 6))
    pick = jnp.where(pick, 1.0, 0.0).astype(BF16)

    def gram_step(v, acc):
        for j in range(4):
            edge = []
            for i in (2 * j, 2 * j + 1):
                p = split(jnp.concatenate([y[v, 2 * i], y[v, 2 * i + 1]], axis=1))
                yp[v, i] = p
                out = lax.dot_general(jnp.concatenate([p, pick], axis=0), p, NT, preferred_element_type=F32)
                acc = acc + out[0 : 2 * S]
                for r in (2 * S, 2 * S + 8):
                    edge.append(out[r : r + 8, 0:S] + out[r : r + 8, S : 2 * S])
            ed[v, j] = jnp.concatenate(edge, axis=1)
        return acc

    acc = lax.fori_loop(0, V, gram_step, jnp.zeros((2 * S, 2 * S), F32))
    start_core(0, pack(acc, tmp))
    radial_halo = [remote(ed, hr.at[0], 2, ahead_r), remote(ed, hr.at[1], 3, behind_r)]
    for h in radial_halo:
        h.start()


    def flux_step(i, carry):
        axial, radial = flux_both([y[v, i] for v in range(V)])
        for v in range(V):
            fs[v, i] = axial[v]
            high = radial[v].astype(BF16)
            gs[v, i, :, 0:NL] = high
            gs[v, i, :, NL : 2 * NL] = (radial[v] - high.astype(F32)).astype(BF16)
        return carry

    lax.fori_loop(0, NI, flux_step, 0)
    tile = end_core(0)
    pl.semaphore_wait(known.at[0], near)
    start_plane(0, tile)
    far = signal(known.at[1], far_z)
    other_halo.start()
    shift = lax.broadcasted_iota(jnp.int32, (NL, NL), 1) - lax.broadcasted_iota(jnp.int32, (NL, NL), 0)
    matrix = jnp.zeros((NL, NL), F32)
    for k, cf in zip((1, 2, 3), COEFFS):
        matrix = jnp.where(shift == k, cf, jnp.where(shift == -k, -cf, matrix))
    matrix = high_low(matrix)
    matrix = jnp.concatenate([matrix, matrix], axis=0)

    def radial_step(v, carry):
        out = jnp.dot(gs[v].reshape(NI * S, 2 * NL), matrix, preferred_element_type=F32)
        dt[v] = (out[:, 0:NL] + out[:, NL : 2 * NL]).reshape(NI, S, NL)
        return carry

    lax.fori_loop(0, V, radial_step, 0)

    for h in radial_halo:
        h.wait()
    step = jnp.where(row8 < 3, row8 + NL - lane8, lane8 + 6 - row8)
    weight = jnp.zeros((8, NL), F32)
    for k, cf in zip((1, 2, 3), COEFFS):
        weight = jnp.where(step == k, cf, weight)
    weight = jnp.where(row8 < 6, jnp.where(row8 < 3, -weight, weight), 0.0)
    weights = high_low(jnp.concatenate([weight] * 16, axis=0))
    group = (lax.broadcasted_iota(jnp.int32, (NL, 2 * NL), 0) // 8) % 8
    valid = jnp.where(row8 < 3, jnp.where(ra < nra - 1, 1, 0), jnp.where((row8 < 6) & (ra > 0), 1, 0)) > 0
    blank = jnp.zeros((24, NL), F32)
    for j in range(4):
        cells = [jnp.where(row8 < 3, hr[1, v, j], hr[0, v, j]) for v in range(V)]
        cells[0] = jnp.where(row8 < 6, cells[0], 1.0)
        rows = jnp.concatenate([jnp.where(valid, g, 0.0) for g in flux_radial(cells)], axis=0)
        high = rows.astype(BF16).astype(F32)
        rows = jnp.concatenate([high, blank, rows - high, blank], axis=0)
        gt[j] = rows.T.astype(BF16)
    for v in range(V):
        out = jnp.dot(gt[...].reshape(NI * S, NL), jnp.where(group == v, weights, 0.0).astype(BF16), preferred_element_type=F32)
        dt[v] = dt[v] + (out[:, 0:NL] + out[:, NL : 2 * NL]).reshape(NI, S, NL)

    def axial_step(v, acc):
        for i in range(NI // 2):
            pair = []
            for r in (2 * i, 2 * i + 1):
                total = dt[v, r]
                for k, cf in zip((1, 2, 3), COEFFS):
                    if r >= k:
                        total = total + cf * fs[v, r - k]
                    if r + k < NI:
                        total = total - cf * fs[v, r + k]
                dt[v, r] = total
                pair.append(total)
            acc = acc + lax.dot_general(yp[v, i], split(jnp.concatenate(pair, axis=1)), NT, preferred_element_type=F32)
        return acc

    acc = lax.fori_loop(0, V, axial_step, jnp.zeros((2 * S, 2 * S), F32))

    def halo_flux(side):
        keep = jnp.full((S, NL), jnp.where(side == 0, jnp.where(sp > 0, 1, 0), jnp.where(sp < nsp - 1, 1, 0))) > 0
        for j in range(3):
            axial = flux_axial([ha[side, v, j] for v in range(V)])
            for v in range(V):
                fh[side, v, j] = jnp.where(keep, axial[v], 0.0)
        return keep

    lower = jnp.where(c == 0, 1.0, 0.0)

    def cross_coeff(mine, theirs):
        if mine == theirs:
            return COEFFS[2]
        if mine < theirs:
            return COEFFS[2 - theirs + mine] * lower
        return COEFFS[2 - mine + theirs] * (1.0 - lower)

    first_halo.wait()
    keep = halo_flux(c)
    sign = 2.0 * lower - 1.0

    def cross_step(v, acc):
        theirs = [fh[c, v, j] for j in range(3)]
        mine = [fs[v, c * (NI - 3) + j] for j in range(3)]
        for p in range(3):
            near_mine = sign * sum(cross_coeff(p, j) * theirs[j] for j in range(3))
            near_theirs = -sign * sum(cross_coeff(j, p) * mine[j] for j in range(3))
            left = jnp.concatenate([y[v, c * (NI - 3) + p], jnp.where(keep, ha[c, v, p], 0.0)], axis=1)
            right = jnp.concatenate([near_mine, near_theirs], axis=1)
            acc = acc + lax.dot_general(split(left), split(right), NT, preferred_element_type=F32)
        return acc

    acc = lax.fori_loop(0, V, cross_step, acc)
    start_core(1, pack(acc, tmp))

    tile = end_plane(0)
    if far:
        pl.semaphore_wait(known.at[1], far)
    start_deep(0, tile)
    start_plane(1, end_core(1))

    other_halo.wait()
    halo_flux(1 - c)
    for v in range(V):
        for p in range(3):
            low_row, high_row = dt[v, p], dt[v, NI - 3 + p]
            for j in range(p, 3):
                low_row = low_row + COEFFS[2 - j + p] * fh[0, v, j]
            for j in range(p + 1):
                high_row = high_row - COEFFS[2 - p + j] * fh[1, v, j]
            dt[v, p], dt[v, NI - 3 + p] = low_row, high_row
    for s in range(S):
        pltpu.make_async_copy(dt.at[:, :, s, :], div.at[s], out_sem.at[0]).start()
    start_deep(1, end_plane(1))
    gram = unpack(end_deep(0)) / count
    low = inverse_factor(gram)

    twice = low + pltpu.roll(low, S, axis=1)
    high = twice.astype(BF16)
    lhs = jnp.concatenate([high, (twice - high.astype(F32)).astype(BF16)], axis=0)[:, 0 : 2 * S]

    def mode_step(v, carry):
        for i in range(NI // 2):
            out = jnp.dot(lhs, yp[v, i], preferred_element_type=F32)
            out = out[0:S] + out[S : 2 * S]
            mt[v, 2 * i], mt[v, 2 * i + 1] = out[:, 0:NL], out[:, NL : 2 * NL]
        return carry

    lax.fori_loop(0, V, mode_step, 0)
    for s in range(S):
        pltpu.make_async_copy(mt.at[:, :, s, :], modes.at[s], out_sem.at[1]).start()
    cross = unpack(end_deep(1))
    root = jnp.sqrt(jnp.full((S, S), count, F32))
    red[...] = jnp.dot(low[:, 0:S], cross[:, 0:S], preferred_element_type=F32, precision=HIGHEST) / root
    pltpu.make_async_copy(dt, dt, out_sem.at[0]).wait()
    pltpu.make_async_copy(mt, mt, out_sem.at[1]).wait()


def write_kernel(modes, div, red, modes_out, div_out, red_out, sem):
    pairs = ((modes, modes_out), (div, div_out), (red, red_out))
    copies = [pltpu.make_async_copy(a, b, sem.at[i]) for i, (a, b) in enumerate(pairs)]
    for copy in copies:
        copy.start()
    for copy in copies:
        copy.wait()


def per_device(dims, snapshots):
    nz, nx, ny = dims
    count = float(V * NI * nz * nx * NL * ny * 2)
    vmem = pl.BlockSpec(memory_space=pltpu.VMEM)
    hbm = pl.BlockSpec(memory_space=pl.ANY)
    big = (S, V, NI, NL)
    dma = pltpu.SemaphoreType.DMA
    modes, div, red = pl.pallas_call(
        functools.partial(main_kernel, dims, count),
        out_shape=[pltpu.VMEM(big, F32), pltpu.VMEM(big, F32), pltpu.VMEM((S, S), F32)],
        in_specs=[hbm],
        out_specs=[vmem, vmem, vmem],
        scratch_shapes=[
            pltpu.VMEM((V, NI, S, NL), F32),
            pltpu.VMEM((V, NI // 2, 2 * S, 2 * NL), BF16),
            pltpu.VMEM((V, NI, S, NL), F32),
            pltpu.VMEM((2, V, 3, S, NL), F32),
            pltpu.VMEM((V, NI, S, NL), F32),
            pltpu.VMEM((V, NI, S, NL), F32),
            pltpu.VMEM((V, NI, S, 2 * NL), BF16),
            pltpu.VMEM((4, NL, NL), BF16),
            pltpu.VMEM((V, 4, 8, NL), F32),
            pltpu.VMEM((2, V, 3, S, NL), F32),
            pltpu.VMEM((2, V, 4, 8, NL), F32),
            pltpu.VMEM((2 * S, NL), F32),
            pltpu.VMEM((6, 8, NL), F32),
            pltpu.VMEM((2, 8, NL), F32),
            pltpu.VMEM((2, nx * ny, 8, NL), F32),
            pltpu.VMEM((2, nz, 8, NL), F32),
            pltpu.SemaphoreType.REGULAR((2,)),
            dma,
            dma((2,)),
            dma((10,)),
            dma((10,)),
        ],
        compiler_params=pltpu.CompilerParams(collective_id=0, has_side_effects=True),
    )(snapshots)
    pinned = [pltpu.with_memory_space_constraint(a, pltpu.VMEM) for a in (modes, div, red)]
    modes, div, red = pl.pallas_call(
        write_kernel,
        out_shape=[jax.ShapeDtypeStruct(big, F32), jax.ShapeDtypeStruct(big, F32), jax.ShapeDtypeStruct((S, S), F32)],
        in_specs=[vmem, vmem, vmem],
        out_specs=[hbm, hbm, hbm],
        scratch_shapes=[dma((3,))],
    )(*pinned)
    return modes, div, red


def solution(mesh):
    space, radial = mesh.shape["space"], mesh.shape["radial"]
    nx = 4 if space > 4 else 2
    placed = P(None, None, "space", "radial")
    return jax.shard_map(
        functools.partial(per_device, (space // nx, nx, radial // 2)),
        mesh=mesh,
        in_specs=(placed,),
        out_specs=(placed, placed, P()),
        check_vma=False,
    )
```

```python
import functools

import jax
import jax.numpy as jnp
from jax import lax
from jax.experimental import pallas as pl
from jax.experimental.pallas import tpu as pltpu
from jax.sharding import PartitionSpec as P

MESH = pl.DeviceIdType.MESH
F32 = jnp.float32
BF16 = jnp.bfloat16
HIGHEST = lax.Precision.HIGHEST
SIXTIETHS = (45.0, -9.0, 1.0)
SCALE = 1.0 / 60.0
S, V, NI, NL = 32, 5, 16, 128
NT = (((1,), (1,)), ((), ()))
TN = (((0,), (0,)), ((), ()))


def split(a):
    high = a.astype(BF16)
    low = (a - high.astype(F32)).astype(BF16)
    return jnp.concatenate([high, low], axis=0)


def parts(a):
    high = a.astype(BF16).astype(F32)
    return high, a - high


def flux_state(q):
    rho, ma, mb, mc, energy = q
    inv = 1.0 / rho
    ua, ub, uc = ma * inv, mb * inv, mc * inv
    press = 0.4 * (energy - 0.5 * (ma * ua + mb * ub + mc * uc))
    return ua, ub, press


def flux_axial(q):
    _, ma, mb, mc, energy = q
    ua, _, press = flux_state(q)
    return (ma, ma * ua + press, mb * ua, mc * ua, (energy + press) * ua)


def flux_radial(q):
    _, ma, mb, mc, energy = q
    _, ub, press = flux_state(q)
    return (mb, ma * ub, mb * ub + press, mc * ub, (energy + press) * ub)


def flux_both(q):
    _, ma, mb, mc, energy = q
    ua, ub, press = flux_state(q)
    cross, total = mb * ua, energy + press
    axial = (ma, ma * ua + press, cross, mc * ua, total * ua)
    radial = (mb, cross, mb * ub + press, mc * ub, total * ub)
    return axial, radial


def pack(acc, tmp, more=None):
    tmp[...] = jnp.zeros_like(tmp)
    tmp[:, 0:64] = acc
    full = tmp[...]
    rows = full[0:32] + full[32:64]
    both = rows + pltpu.roll(rows, NL - 32, axis=1)
    if more is not None:
        both = both + more[0:S]
        for r in (1, 2, 3):
            both = both + pltpu.roll(more[S * r : S * (r + 1)], NL - S * r, axis=1)
        both = both * SCALE
    lane = lax.broadcasted_iota(jnp.int32, (8, NL), 1)
    out = jnp.zeros((8, NL), F32)
    for r in range(4):
        part = both[8 * r : 8 * r + 8]
        if r:
            part = pltpu.roll(part, 32 * r, axis=1)
        out = jnp.where(lane // 32 == r, part, out)
    return out


def unpack(tile):
    return jnp.concatenate([tile] + [pltpu.roll(tile, NL - 32 * r, axis=1) for r in (1, 2, 3)], axis=0)


def inverse_factor(gram):
    row = lax.broadcasted_iota(jnp.int32, (S, NL), 0)
    lane = lax.broadcasted_iota(jnp.int32, (S, NL), 1)
    w = jnp.where(lane < S, gram, jnp.where(lane == row + S, 1.0, 0.0))
    for k in range(S - 1):
        pivot = w[k : k + 1, :]
        scale = w[:, k : k + 1] * (1.0 / w[k : k + 1, k : k + 1])
        w = w - jnp.where(row > k, scale, 0.0) * pivot
    diag = jnp.sum(jnp.where(lane == row, w, 0.0), axis=1, keepdims=True)
    low = pltpu.roll(w, NL - S, axis=1) * lax.rsqrt(diag)
    return jnp.where(lane < S, low, 0.0)


def offsets(n, steps):
    return sorted({d % n for k in steps for d in (k, -k)} - {0})


def main_kernel(dims, count, snap, modes, div, red, y, yp, fs, fh, dt, mt, gs, gt, gz, ed, ha, hr, tmp, sb, rc, rp, rz, known, load_sem, out_sem, send, recv):
    nz, nx, ny = dims
    nsp, nra = nz * nx, ny * 2
    sp, ra = lax.axis_index("space"), lax.axis_index("radial")
    z, x = sp // nx, sp % nx
    yy, c = ra // 2, ra % 2
    def plane(o):
        return (z * nx + (x + o[0]) % nx, ((yy + o[1]) % ny) * 2 + c)

    def deep(d):
        return (((z + d) % nz) * nx + x, ra)

    def nth_plane(n):
        half_x, half_y = nx // 2, ny // 2
        own = (nx - half_x) % nx * ny + (ny - half_y) % ny
        n = jnp.where(n >= own, n + 1, n)
        return plane((half_x + n // ny, half_y + n % ny))

    def nth_deep(n):
        return deep(nz // 2 + jnp.where(n % 2 == 1, nz - (n + 1) // 2, n // 2))

    core = (sp, yy * 2 + 1 - c)
    ahead_a, behind_a = ((sp + 1) % nsp, ra), ((sp + nsp - 1) % nsp, ra)
    ahead_r, behind_r = (sp, (ra + 1) % nra), (sp, (ra + nra - 1) % nra)

    barrier = pltpu.get_barrier_semaphore()
    line_x, line_y = [plane((d, 0)) for d in range(1, nx)], [plane((0, d)) for d in range(1, ny)]
    near_z, skip_z, far_z = [[deep(d) for d in offsets(nz, n)] for n in ((1, 2), (2,), (4,))]

    def signal(semaphore, targets):
        for peer in targets:
            pl.semaphore_signal(semaphore, inc=1, device_id=peer, device_id_type=MESH)
        return len(targets)

    near = signal(barrier, [ahead_a, behind_a, ahead_r, behind_r, core] + near_z + line_x + line_y)
    for s in range(S):
        pltpu.make_async_copy(snap.at[s], y.at[:, :, s, :], load_sem).start()
    pltpu.make_async_copy(y, y, load_sem).wait()
    pl.semaphore_wait(barrier, near)

    def remote(src, dst, k, peer):
        return pltpu.make_async_remote_copy(src, dst, send.at[k], recv.at[k], device_id=peer, device_id_type=MESH)

    first_halo = remote(y.at[:, pl.ds((1 - c) * (NI - 3), 3)], ha.at[c], 0, ((sp + nsp + 1 - 2 * c) % nsp, ra))
    other_halo = remote(y.at[:, pl.ds(c * (NI - 3), 3)], ha.at[1 - c], 1, ((sp + nsp - 1 + 2 * c) % nsp, ra))
    has_behind, has_ahead = jnp.where(sp > 0, 1, 0), jnp.where(sp < nsp - 1, 1, 0)
    first_sent = jnp.where(c == 0, has_ahead, has_behind) > 0
    first_due = jnp.where(c == 0, has_behind, has_ahead) > 0

    @pl.when(first_sent)
    def _():
        first_halo.start()

    near = signal(known.at[0], line_x + skip_z)

    def start_core(k, tile):
        sb[3 * k] = tile
        remote(sb.at[3 * k], rc.at[k], 4 + 3 * k, core).start()

    def end_core(k):
        remote(sb.at[3 * k], rc.at[k], 4 + 3 * k, core).wait()
        return sb[3 * k] + rc[k]

    def start_many(k, stage, buf, mine, n, target, tile):
        sb[3 * k + stage] = tile
        buf[k, mine] = tile

        def send_one(i, carry):
            remote(sb.at[3 * k + stage], buf.at[k, mine], 4 + 3 * k + stage, target(i)).start()
            return carry

        lax.fori_loop(0, n - 1, send_one, 0)

    def end_many(k, stage, buf, n):
        landed = buf.at[k, 0 : n - 1]
        pltpu.make_async_copy(landed, landed, recv.at[4 + 3 * k + stage]).wait()
        pltpu.make_async_copy(landed, landed, send.at[4 + 3 * k + stage]).wait()
        terms = [buf[k, i] for i in range(n)]
        while len(terms) > 1:
            terms = [terms[i] + terms[i + 1] for i in range(0, len(terms), 2)]
        return terms[0]

    def start_plane(k, tile):
        start_many(k, 1, rp, x * ny + yy, nx * ny, nth_plane, tile)

    def end_plane(k):
        return end_many(k, 1, rp, nx * ny)

    def start_deep(k, tile):
        start_many(k, 2, rz, z, nz, nth_deep, tile)

    def end_deep(k):
        return end_many(k, 2, rz, nz)

    row8 = lax.broadcasted_iota(jnp.int32, (8, NL), 0)
    lane8 = lax.broadcasted_iota(jnp.int32, (8, NL), 1)
    row16 = lax.broadcasted_iota(jnp.int32, (16, 2 * NL), 0)
    lane16 = lax.broadcasted_iota(jnp.int32, (16, 2 * NL), 1)
    cell = row16 % 8
    pick = (cell < 6) & (lane16 == row16 // 8 * NL + jnp.where(cell < 3, cell, cell + NL - 6))
    pick = jnp.where(pick, 1.0, 0.0).astype(BF16)

    def gram_step(v, acc):
        for j in range(4):
            edge = []
            for i in (2 * j, 2 * j + 1):
                p = split(jnp.concatenate([y[v, 2 * i], y[v, 2 * i + 1]], axis=1))
                yp[v, i] = p
                out = lax.dot_general(jnp.concatenate([p, pick], axis=0), p, NT, preferred_element_type=F32)
                acc = acc + out[0 : 2 * S]
                for r in (2 * S, 2 * S + 8):
                    edge.append(out[r : r + 8, 0:S] + out[r : r + 8, S : 2 * S])
            ed[v, j] = jnp.concatenate(edge, axis=1)
        return acc

    acc = lax.fori_loop(0, V, gram_step, jnp.zeros((2 * S, 2 * S), F32))
    start_core(0, pack(acc, tmp))
    radial_halo = [remote(ed, hr.at[0], 2, ahead_r), remote(ed, hr.at[1], 3, behind_r)]
    for h in radial_halo:
        h.start()


    def flux_step(i, carry):
        axial, radial = flux_both([y[v, i] for v in range(V)])
        for v in range(V):
            fs[v, i] = axial[v]
            high = radial[v].astype(BF16)
            gs[v, i, :, 0:NL] = high
            gs[v, i, :, NL : 2 * NL] = (radial[v] - high.astype(F32)).astype(BF16)
        return carry

    lax.fori_loop(0, NI, flux_step, 0)
    tile = end_core(0)
    pl.semaphore_wait(known.at[0], near)
    start_plane(0, tile)
    far = signal(known.at[1], far_z)

    @pl.when(first_due)
    def _():
        other_halo.start()

    shift = lax.broadcasted_iota(jnp.int32, (NL, NL), 1) - lax.broadcasted_iota(jnp.int32, (NL, NL), 0)
    matrix = jnp.zeros((NL, NL), F32)
    for k, cf in zip((1, 2, 3), SIXTIETHS):
        matrix = jnp.where(shift == k, cf, jnp.where(shift == -k, -cf, matrix))
    matrix = jnp.concatenate([matrix, matrix], axis=0).astype(BF16)

    def radial_step(v, carry):
        out = jnp.dot(gs[v].reshape(NI * S, 2 * NL), matrix, preferred_element_type=F32)
        dt[v] = out.reshape(NI, S, NL)
        return carry

    lax.fori_loop(0, V, radial_step, 0)

    def axial_step(v, acc):
        for i in range(NI // 2):
            pair = []
            for r in (2 * i, 2 * i + 1):
                total = dt[v, r]
                for k, cf in zip((1, 2, 3), SIXTIETHS):
                    if k <= r < NI - k:
                        total = total + cf * (fs[v, r - k] - fs[v, r + k])
                    else:
                        total = total + cf * fs[v, r - k] if r >= k else total - cf * fs[v, r + k]
                dt[v, r] = total
                pair.append(total)
            acc = acc + lax.dot_general(yp[v, i], split(jnp.concatenate(pair, axis=1)), NT, preferred_element_type=F32)
        return acc

    acc = lax.fori_loop(0, V, axial_step, jnp.zeros((2 * S, 2 * S), F32))

    def halo_flux(side):
        keep = jnp.full((S, NL), jnp.where(side == 0, jnp.where(sp > 0, 1, 0), jnp.where(sp < nsp - 1, 1, 0))) > 0
        for j in range(3):
            axial = flux_axial([ha[side, v, j] for v in range(V)])
            for v in range(V):
                fh[side, v, j] = jnp.where(keep, axial[v], 0.0)
        return keep

    lower = jnp.where(c == 0, 1.0, 0.0)

    def cross_coeff(mine, theirs):
        if mine == theirs:
            return SIXTIETHS[2]
        if mine < theirs:
            return SIXTIETHS[2 - theirs + mine] * lower
        return SIXTIETHS[2 - mine + theirs] * (1.0 - lower)

    def land(copy, due, side):
        @pl.when(due)
        def _():
            copy.wait_recv()

        @pl.when(jnp.logical_not(due))
        def _():
            ha[side] = jnp.ones((V, 3, S, NL), F32)

    land(first_halo, first_due, c)
    keep = halo_flux(c)
    sign = 2.0 * lower - 1.0

    def cross_step(v, acc):
        theirs = [fh[c, v, j] for j in range(3)]
        mine = [fs[v, c * (NI - 3) + j] for j in range(3)]
        for p in range(3):
            near_mine = sign * sum(cross_coeff(p, j) * theirs[j] for j in range(3))
            near_theirs = -sign * sum(cross_coeff(j, p) * mine[j] for j in range(3))
            left = jnp.concatenate([y[v, c * (NI - 3) + p], jnp.where(keep, ha[c, v, p], 0.0)], axis=1)
            right = jnp.concatenate([near_mine, near_theirs], axis=1)
            acc = acc + lax.dot_general(split(left), split(right), NT, preferred_element_type=F32)
        return acc

    acc = lax.fori_loop(0, V, cross_step, acc)

    for h in radial_halo:
        h.wait()
    edge = lax.broadcasted_iota(jnp.int32, (8 * V, 8 * V), 0)
    ghost = lax.broadcasted_iota(jnp.int32, (8 * V, 8 * V), 1)
    same, edge, ghost = edge // 8 == ghost // 8, edge % 8, ghost % 8
    high_side = jnp.where((ghost < 3) & (edge >= 3) & (edge < 6), 6 + ghost - edge, 0)
    low_side = jnp.where((ghost >= 3) & (ghost < 6) & (edge < 3), 6 + edge - ghost, 0)
    link = jnp.zeros((8 * V, 8 * V), F32)
    for k, cf in zip((1, 2, 3), SIXTIETHS):
        link = jnp.where(same & (low_side == k), cf, jnp.where(same & (high_side == k), -cf, link))
    valid = jnp.where(row8 < 3, jnp.where(ra < nra - 1, 1, 0), jnp.where((row8 < 6) & (ra > 0), 1, 0)) > 0
    blank = jnp.zeros((8, NL), F32)
    more = jnp.zeros((NL, NL), F32)
    for j in range(4):
        cells = [jnp.where(row8 < 3, hr[1, v, j], hr[0, v, j]) for v in range(V)]
        cells[0] = jnp.where(row8 < 6, cells[0], 1.0)
        ghosts = jnp.concatenate([jnp.where(valid, g, 0.0) for g in flux_radial(cells)], axis=0)
        gz[j] = ghosts
        added = parts(jnp.dot(link, ghosts, preferred_element_type=F32, precision=HIGHEST))
        mine = parts(jnp.concatenate([ed[v, j] for v in range(V)], axis=0))
        left = jnp.concatenate([a for m in (0, 1, 0, 1) for a in (mine[m], blank)], axis=0)
        right = jnp.concatenate([a for m in (0, 0, 1, 1) for a in (added[m], blank)], axis=0)
        more = more + lax.dot_general(left.astype(BF16), right.astype(BF16), TN, preferred_element_type=F32)
    start_core(1, pack(acc, tmp, more))

    tile = end_plane(0)
    if far:
        pl.semaphore_wait(known.at[1], far)
    start_deep(0, tile)
    start_plane(1, end_core(1))

    step = jnp.where(row8 < 3, row8 + NL - lane8, lane8 + 6 - row8)
    weight = jnp.zeros((8, NL), F32)
    for k, cf in zip((1, 2, 3), SIXTIETHS):
        weight = jnp.where(step == k, cf, weight)
    weight = jnp.where(row8 < 6, jnp.where(row8 < 3, -weight, weight), 0.0)
    weights = jnp.concatenate([weight] * 16, axis=0)
    group = (lax.broadcasted_iota(jnp.int32, (NL, NL), 0) // 8) % 8
    blank = jnp.zeros((24, NL), F32)
    for j in range(4):
        high, low = parts(gz[j])
        gt[j] = jnp.concatenate([high, blank, low, blank], axis=0).T.astype(BF16)
    for v in range(V):
        out = jnp.dot(gt[...].reshape(NI * S, NL), jnp.where(group == v, weights, 0.0).astype(BF16), preferred_element_type=F32)
        dt[v] = (dt[v] + out.reshape(NI, S, NL)) * SCALE

    land(other_halo, first_sent, 1 - c)
    halo_flux(1 - c)

    @pl.when(first_sent)
    def _():
        first_halo.wait_send()

    @pl.when(first_due)
    def _():
        other_halo.wait_send()

    for v in range(V):
        for p in range(3):
            low_row, high_row = dt[v, p], dt[v, NI - 3 + p]
            for j in range(p, 3):
                low_row = low_row + SCALE * SIXTIETHS[2 - j + p] * fh[0, v, j]
            for j in range(p + 1):
                high_row = high_row - SCALE * SIXTIETHS[2 - p + j] * fh[1, v, j]
            dt[v, p], dt[v, NI - 3 + p] = low_row, high_row
    for s in range(S):
        pltpu.make_async_copy(dt.at[:, :, s, :], div.at[s], out_sem.at[0]).start()
    start_deep(1, end_plane(1))
    gram = unpack(end_deep(0)) / count
    low = inverse_factor(gram)

    twice = low + pltpu.roll(low, S, axis=1)
    high = twice.astype(BF16)
    lhs = jnp.concatenate([high, (twice - high.astype(F32)).astype(BF16)], axis=0)[:, 0 : 2 * S]

    def mode_step(v, carry):
        for i in range(NI // 2):
            out = jnp.dot(lhs, yp[v, i], preferred_element_type=F32)
            out = out[0:S] + out[S : 2 * S]
            mt[v, 2 * i], mt[v, 2 * i + 1] = out[:, 0:NL], out[:, NL : 2 * NL]
        return carry

    lax.fori_loop(0, V, mode_step, 0)
    for s in range(S):
        pltpu.make_async_copy(mt.at[:, :, s, :], modes.at[s], out_sem.at[1]).start()
    cross = unpack(end_deep(1))
    root = jnp.sqrt(jnp.full((S, S), count, F32))
    red[...] = jnp.dot(low[:, 0:S], cross[:, 0:S], preferred_element_type=F32, precision=HIGHEST) / root
    pltpu.make_async_copy(dt, dt, out_sem.at[0]).wait()
    pltpu.make_async_copy(mt, mt, out_sem.at[1]).wait()


def write_kernel(modes, div, red, modes_out, div_out, red_out, sem):
    pairs = ((modes, modes_out), (div, div_out), (red, red_out))
    copies = [pltpu.make_async_copy(a, b, sem.at[i]) for i, (a, b) in enumerate(pairs)]
    for copy in copies:
        copy.start()
    for copy in copies:
        copy.wait()


def per_device(dims, snapshots):
    nz, nx, ny = dims
    count = float(V * NI * nz * nx * NL * ny * 2)
    vmem = pl.BlockSpec(memory_space=pltpu.VMEM)
    hbm = pl.BlockSpec(memory_space=pl.ANY)
    big = (S, V, NI, NL)
    dma = pltpu.SemaphoreType.DMA
    modes, div, red = pl.pallas_call(
        functools.partial(main_kernel, dims, count),
        out_shape=[pltpu.VMEM(big, F32), pltpu.VMEM(big, F32), pltpu.VMEM((S, S), F32)],
        in_specs=[hbm],
        out_specs=[vmem, vmem, vmem],
        scratch_shapes=[
            pltpu.VMEM((V, NI, S, NL), F32),
            pltpu.VMEM((V, NI // 2, 2 * S, 2 * NL), BF16),
            pltpu.VMEM((V, NI, S, NL), F32),
            pltpu.VMEM((2, V, 3, S, NL), F32),
            pltpu.VMEM((V, NI, S, NL), F32),
            pltpu.VMEM((V, NI, S, NL), F32),
            pltpu.VMEM((V, NI, S, 2 * NL), BF16),
            pltpu.VMEM((4, NL, NL), BF16),
            pltpu.VMEM((4, 8 * V, NL), F32),
            pltpu.VMEM((V, 4, 8, NL), F32),
            pltpu.VMEM((2, V, 3, S, NL), F32),
            pltpu.VMEM((2, V, 4, 8, NL), F32),
            pltpu.VMEM((2 * S, NL), F32),
            pltpu.VMEM((6, 8, NL), F32),
            pltpu.VMEM((2, 8, NL), F32),
            pltpu.VMEM((2, nx * ny, 8, NL), F32),
            pltpu.VMEM((2, nz, 8, NL), F32),
            pltpu.SemaphoreType.REGULAR((2,)),
            dma,
            dma((2,)),
            dma((10,)),
            dma((10,)),
        ],
        compiler_params=pltpu.CompilerParams(collective_id=0, has_side_effects=True),
    )(snapshots)
    pinned = [pltpu.with_memory_space_constraint(a, pltpu.VMEM) for a in (modes, div, red)]
    modes, div, red = pl.pallas_call(
        write_kernel,
        out_shape=[jax.ShapeDtypeStruct(big, F32), jax.ShapeDtypeStruct(big, F32), jax.ShapeDtypeStruct((S, S), F32)],
        in_specs=[vmem, vmem, vmem],
        out_specs=[hbm, hbm, hbm],
        scratch_shapes=[dma((3,))],
    )(*pinned)
    return modes, div, red


def solution(mesh):
    space, radial = mesh.shape["space"], mesh.shape["radial"]
    nx = 4 if space > 4 else 2
    placed = P(None, None, "space", "radial")
    return jax.shard_map(
        functools.partial(per_device, (space // nx, nx, radial // 2)),
        mesh=mesh,
        in_specs=(placed,),
        out_specs=(placed, placed, P()),
        check_vma=False,
    )
```

```python
import functools

import jax
import jax.numpy as jnp
from jax import lax
from jax.experimental import pallas as pl
from jax.experimental.pallas import tpu as pltpu
from jax.sharding import PartitionSpec as P

MESH = pl.DeviceIdType.MESH
F32 = jnp.float32
BF16 = jnp.bfloat16
HIGHEST = lax.Precision.HIGHEST
SIXTIETHS = (45.0, -9.0, 1.0)
SCALE = 1.0 / 60.0
S, V, NI, NL = 32, 5, 16, 128
NT = (((1,), (1,)), ((), ()))
TN = (((0,), (0,)), ((), ()))


def split(a):
    high = a.astype(BF16)
    low = (a - high.astype(F32)).astype(BF16)
    return jnp.concatenate([high, low], axis=0)


def parts(a):
    high = a.astype(BF16).astype(F32)
    return high, a - high


def flux_state(q):
    rho, ma, mb, mc, energy = q
    inv = 1.0 / rho
    ua, ub, uc = ma * inv, mb * inv, mc * inv
    press = 0.4 * (energy - 0.5 * (ma * ua + mb * ub + mc * uc))
    return ua, ub, press


def flux_axial(q):
    _, ma, mb, mc, energy = q
    ua, _, press = flux_state(q)
    return (ma, ma * ua + press, mb * ua, mc * ua, (energy + press) * ua)


def flux_radial(q):
    _, ma, mb, mc, energy = q
    _, ub, press = flux_state(q)
    return (mb, ma * ub, mb * ub + press, mc * ub, (energy + press) * ub)


def flux_both(q):
    _, ma, mb, mc, energy = q
    ua, ub, press = flux_state(q)
    cross, total = mb * ua, energy + press
    axial = (ma, ma * ua + press, cross, mc * ua, total * ua)
    radial = (mb, cross, mb * ub + press, mc * ub, total * ub)
    return axial, radial


def pack(acc, tmp, more=None):
    tmp[...] = jnp.zeros_like(tmp)
    tmp[:, 0:64] = acc
    full = tmp[...]
    rows = full[0:32] + full[32:64]
    both = rows + pltpu.roll(rows, NL - 32, axis=1)
    if more is not None:
        both = both + more[0:S]
        for r in (1, 2, 3):
            both = both + pltpu.roll(more[S * r : S * (r + 1)], NL - S * r, axis=1)
        both = both * SCALE
    lane = lax.broadcasted_iota(jnp.int32, (8, NL), 1)
    out = jnp.zeros((8, NL), F32)
    for r in range(4):
        part = both[8 * r : 8 * r + 8]
        if r:
            part = pltpu.roll(part, 32 * r, axis=1)
        out = jnp.where(lane // 32 == r, part, out)
    return out


def unpack(tile):
    return jnp.concatenate([tile] + [pltpu.roll(tile, NL - 32 * r, axis=1) for r in (1, 2, 3)], axis=0)


def inverse_factor(gram):
    row = lax.broadcasted_iota(jnp.int32, (S, NL), 0)
    lane = lax.broadcasted_iota(jnp.int32, (S, NL), 1)
    w = jnp.where(lane < S, gram, jnp.where(lane == row + S, 1.0, 0.0))
    for k in range(S - 1):
        pivot = w[k : k + 1, :]
        scale = w[:, k : k + 1] * (1.0 / w[k : k + 1, k : k + 1])
        w = w - jnp.where(row > k, scale, 0.0) * pivot
    diag = jnp.sum(jnp.where(lane == row, w, 0.0), axis=1, keepdims=True)
    low = pltpu.roll(w, NL - S, axis=1) * lax.rsqrt(diag)
    return jnp.where(lane < S, low, 0.0)


def offsets(n, steps):
    return sorted({d % n for k in steps for d in (k, -k)} - {0})


def main_kernel(dims, count, snap, modes, div, red, y, yp, fs, fh, dt, gs, gt, gz, ed, ha, hr, tmp, sb, rc, rp, rz, known, load_sem, send, recv):
    nz, nx, ny = dims
    nsp, nra = nz * nx, ny * 2
    sp, ra = lax.axis_index("space"), lax.axis_index("radial")
    z, x = sp // nx, sp % nx
    yy, c = ra // 2, ra % 2
    def plane(o):
        return (z * nx + (x + o[0]) % nx, ((yy + o[1]) % ny) * 2 + c)

    def deep(d):
        return (((z + d) % nz) * nx + x, ra)

    def nth_plane(n):
        half_x, half_y = nx // 2, ny // 2
        own = (nx - half_x) % nx * ny + (ny - half_y) % ny
        n = jnp.where(n >= own, n + 1, n)
        return plane((half_x + n // ny, half_y + n % ny))

    def nth_deep(n):
        return deep(nz // 2 + jnp.where(n % 2 == 1, nz - (n + 1) // 2, n // 2))

    core = (sp, yy * 2 + 1 - c)
    ahead_a, behind_a = ((sp + 1) % nsp, ra), ((sp + nsp - 1) % nsp, ra)
    ahead_r, behind_r = (sp, (ra + 1) % nra), (sp, (ra + nra - 1) % nra)

    barrier = pltpu.get_barrier_semaphore()
    line_x, line_y = [plane((d, 0)) for d in range(1, nx)], [plane((0, d)) for d in range(1, ny)]
    near_z, skip_z, far_z = [[deep(d) for d in offsets(nz, n)] for n in ((1, 2), (2,), (4,))]

    def signal(semaphore, targets):
        for peer in targets:
            pl.semaphore_signal(semaphore, inc=1, device_id=peer, device_id_type=MESH)
        return len(targets)

    near = signal(barrier, [ahead_a, behind_a, ahead_r, behind_r, core] + near_z + line_x + line_y)
    for s in range(S):
        pltpu.make_async_copy(snap.at[s], y.at[:, :, s, :], load_sem).start()
    pltpu.make_async_copy(y, y, load_sem).wait()
    pl.semaphore_wait(barrier, near)

    def remote(src, dst, k, peer):
        return pltpu.make_async_remote_copy(src, dst, send.at[k], recv.at[k], device_id=peer, device_id_type=MESH)

    first_halo = remote(y.at[:, pl.ds((1 - c) * (NI - 3), 3)], ha.at[c], 0, ((sp + nsp + 1 - 2 * c) % nsp, ra))
    other_halo = remote(y.at[:, pl.ds(c * (NI - 3), 3)], ha.at[1 - c], 1, ((sp + nsp - 1 + 2 * c) % nsp, ra))
    has_behind, has_ahead = jnp.where(sp > 0, 1, 0), jnp.where(sp < nsp - 1, 1, 0)
    first_sent = jnp.where(c == 0, has_ahead, has_behind) > 0
    first_due = jnp.where(c == 0, has_behind, has_ahead) > 0

    @pl.when(first_sent)
    def _():
        first_halo.start()

    @pl.when(first_due)
    def _():
        other_halo.start()

    near = signal(known.at[0], line_x + skip_z)

    def start_core(k, tile):
        sb[3 * k] = tile
        remote(sb.at[3 * k], rc.at[k], 4 + 3 * k, core).start()

    def end_core(k):
        remote(sb.at[3 * k], rc.at[k], 4 + 3 * k, core).wait()
        return sb[3 * k] + rc[k]

    def start_many(k, stage, buf, mine, n, target, tile):
        sb[3 * k + stage] = tile
        buf[k, mine] = tile

        def send_one(i, carry):
            remote(sb.at[3 * k + stage], buf.at[k, mine], 4 + 3 * k + stage, target(i)).start()
            return carry

        lax.fori_loop(0, n - 1, send_one, 0)

    def end_many(k, stage, buf, n):
        landed = buf.at[k, 0 : n - 1]
        pltpu.make_async_copy(landed, landed, recv.at[4 + 3 * k + stage]).wait()
        pltpu.make_async_copy(landed, landed, send.at[4 + 3 * k + stage]).wait()
        terms = [buf[k, i] for i in range(n)]
        while len(terms) > 1:
            terms = [terms[i] + terms[i + 1] for i in range(0, len(terms), 2)]
        return terms[0]

    def start_plane(k, tile):
        start_many(k, 1, rp, x * ny + yy, nx * ny, nth_plane, tile)

    def end_plane(k):
        return end_many(k, 1, rp, nx * ny)

    def start_deep(k, tile):
        start_many(k, 2, rz, z, nz, nth_deep, tile)

    def end_deep(k):
        return end_many(k, 2, rz, nz)

    row8 = lax.broadcasted_iota(jnp.int32, (8, NL), 0)
    lane8 = lax.broadcasted_iota(jnp.int32, (8, NL), 1)
    row16 = lax.broadcasted_iota(jnp.int32, (16, 2 * NL), 0)
    lane16 = lax.broadcasted_iota(jnp.int32, (16, 2 * NL), 1)
    cell = row16 % 8
    pick = (cell < 6) & (lane16 == row16 // 8 * NL + jnp.where(cell < 3, cell, cell + NL - 6))
    pick = jnp.where(pick, 1.0, 0.0).astype(BF16)

    def gram_step(v, acc):
        for j in range(4):
            edge = []
            for i in (2 * j, 2 * j + 1):
                p = split(jnp.concatenate([y[v, 2 * i], y[v, 2 * i + 1]], axis=1))
                yp[v, i] = p
                out = lax.dot_general(jnp.concatenate([p, pick], axis=0), p, NT, preferred_element_type=F32)
                acc = acc + out[0 : 2 * S]
                for r in (2 * S, 2 * S + 8):
                    edge.append(out[r : r + 8, 0:S] + out[r : r + 8, S : 2 * S])
            ed[v, j] = jnp.concatenate(edge, axis=1)
        return acc

    acc = lax.fori_loop(0, V, gram_step, jnp.zeros((2 * S, 2 * S), F32))
    start_core(0, pack(acc, tmp))
    radial_halo = [remote(ed, hr.at[0], 2, ahead_r), remote(ed, hr.at[1], 3, behind_r)]
    for h in radial_halo:
        h.start()


    def flux_step(i, carry):
        axial, radial = flux_both([y[v, i] for v in range(V)])
        for v in range(V):
            fs[v, i] = axial[v]
            high = radial[v].astype(BF16)
            gs[v, i, :, 0:NL] = high
            gs[v, i, :, NL : 2 * NL] = (radial[v] - high.astype(F32)).astype(BF16)
        return carry

    lax.fori_loop(0, NI, flux_step, 0)
    tile = end_core(0)
    pl.semaphore_wait(known.at[0], near)
    start_plane(0, tile)
    far = signal(known.at[1], far_z)
    shift = lax.broadcasted_iota(jnp.int32, (NL, NL), 1) - lax.broadcasted_iota(jnp.int32, (NL, NL), 0)
    matrix = jnp.zeros((NL, NL), F32)
    for k, cf in zip((1, 2, 3), SIXTIETHS):
        matrix = jnp.where(shift == k, cf, jnp.where(shift == -k, -cf, matrix))
    matrix = jnp.concatenate([matrix, matrix], axis=0).astype(BF16)

    def radial_step(v, carry):
        out = jnp.dot(gs[v].reshape(NI * S, 2 * NL), matrix, preferred_element_type=F32)
        dt[v] = out.reshape(NI, S, NL)
        return carry

    lax.fori_loop(0, V, radial_step, 0)

    def axial_step(v, acc):
        for i in range(NI // 2):
            pair = []
            for r in (2 * i, 2 * i + 1):
                total = dt[v, r]
                for k, cf in zip((1, 2, 3), SIXTIETHS):
                    if k <= r < NI - k:
                        total = total + cf * (fs[v, r - k] - fs[v, r + k])
                    else:
                        total = total + cf * fs[v, r - k] if r >= k else total - cf * fs[v, r + k]
                dt[v, r] = total
                pair.append(total)
            acc = acc + lax.dot_general(yp[v, i], split(jnp.concatenate(pair, axis=1)), NT, preferred_element_type=F32)
        return acc

    acc = lax.fori_loop(0, V, axial_step, jnp.zeros((2 * S, 2 * S), F32))

    def halo_flux(side):
        keep = jnp.full((S, NL), jnp.where(side == 0, jnp.where(sp > 0, 1, 0), jnp.where(sp < nsp - 1, 1, 0))) > 0
        for j in range(3):
            axial = flux_axial([ha[side, v, j] for v in range(V)])
            for v in range(V):
                fh[side, v, j] = jnp.where(keep, axial[v], 0.0)
        return keep

    lower = jnp.where(c == 0, 1.0, 0.0)

    def cross_coeff(mine, theirs):
        if mine == theirs:
            return SIXTIETHS[2]
        if mine < theirs:
            return SIXTIETHS[2 - theirs + mine] * lower
        return SIXTIETHS[2 - mine + theirs] * (1.0 - lower)

    def land(copy, due, side):
        @pl.when(due)
        def _():
            copy.wait_recv()

        @pl.when(jnp.logical_not(due))
        def _():
            ha[side] = jnp.ones((V, 3, S, NL), F32)

    land(first_halo, first_due, c)
    keep = halo_flux(c)
    sign = 2.0 * lower - 1.0

    def cross_step(v, acc):
        theirs = [fh[c, v, j] for j in range(3)]
        mine = [fs[v, c * (NI - 3) + j] for j in range(3)]
        for p in range(3):
            near_mine = sign * sum(cross_coeff(p, j) * theirs[j] for j in range(3))
            near_theirs = -sign * sum(cross_coeff(j, p) * mine[j] for j in range(3))
            left = jnp.concatenate([y[v, c * (NI - 3) + p], jnp.where(keep, ha[c, v, p], 0.0)], axis=1)
            right = jnp.concatenate([near_mine, near_theirs], axis=1)
            acc = acc + lax.dot_general(split(left), split(right), NT, preferred_element_type=F32)
        return acc

    acc = lax.fori_loop(0, V, cross_step, acc)

    for h in radial_halo:
        h.wait()
    edge = lax.broadcasted_iota(jnp.int32, (8 * V, 8 * V), 0)
    ghost = lax.broadcasted_iota(jnp.int32, (8 * V, 8 * V), 1)
    same, edge, ghost = edge // 8 == ghost // 8, edge % 8, ghost % 8
    high_side = jnp.where((ghost < 3) & (edge >= 3) & (edge < 6), 6 + ghost - edge, 0)
    low_side = jnp.where((ghost >= 3) & (ghost < 6) & (edge < 3), 6 + edge - ghost, 0)
    link = jnp.zeros((8 * V, 8 * V), F32)
    for k, cf in zip((1, 2, 3), SIXTIETHS):
        link = jnp.where(same & (low_side == k), cf, jnp.where(same & (high_side == k), -cf, link))
    valid = jnp.where(row8 < 3, jnp.where(ra < nra - 1, 1, 0), jnp.where((row8 < 6) & (ra > 0), 1, 0)) > 0
    blank = jnp.zeros((8, NL), F32)
    more = jnp.zeros((NL, NL), F32)
    for j in range(4):
        cells = [jnp.where(row8 < 3, hr[1, v, j], hr[0, v, j]) for v in range(V)]
        cells[0] = jnp.where(row8 < 6, cells[0], 1.0)
        ghosts = jnp.concatenate([jnp.where(valid, g, 0.0) for g in flux_radial(cells)], axis=0)
        gz[j] = ghosts
        added = parts(jnp.dot(link, ghosts, preferred_element_type=F32, precision=HIGHEST))
        mine = parts(jnp.concatenate([ed[v, j] for v in range(V)], axis=0))
        left = jnp.concatenate([a for m in (0, 1, 0, 1) for a in (mine[m], blank)], axis=0)
        right = jnp.concatenate([a for m in (0, 0, 1, 1) for a in (added[m], blank)], axis=0)
        more = more + lax.dot_general(left.astype(BF16), right.astype(BF16), TN, preferred_element_type=F32)
    start_core(1, pack(acc, tmp, more))

    tile = end_plane(0)
    if far:
        pl.semaphore_wait(known.at[1], far)
    start_deep(0, tile)
    start_plane(1, end_core(1))

    step = jnp.where(row8 < 3, row8 + NL - lane8, lane8 + 6 - row8)
    weight = jnp.zeros((8, NL), F32)
    for k, cf in zip((1, 2, 3), SIXTIETHS):
        weight = jnp.where(step == k, cf, weight)
    weight = jnp.where(row8 < 6, jnp.where(row8 < 3, -weight, weight), 0.0)
    weights = jnp.concatenate([weight] * 16, axis=0)
    group = (lax.broadcasted_iota(jnp.int32, (NL, NL), 0) // 8) % 8
    blank = jnp.zeros((24, NL), F32)
    for j in range(4):
        high, low = parts(gz[j])
        gt[j] = jnp.concatenate([high, blank, low, blank], axis=0).T.astype(BF16)
    for v in range(V):
        out = jnp.dot(gt[...].reshape(NI * S, NL), jnp.where(group == v, weights, 0.0).astype(BF16), preferred_element_type=F32)
        dt[v] = (dt[v] + out.reshape(NI, S, NL)) * SCALE
        for i in range(3, NI - 3):
            div[pl.ds(v * NI + i, S, stride=V * NI), :] = dt[v, i]

    land(other_halo, first_sent, 1 - c)
    halo_flux(1 - c)

    @pl.when(first_sent)
    def _():
        first_halo.wait_send()

    @pl.when(first_due)
    def _():
        other_halo.wait_send()

    for v in range(V):
        for p in range(3):
            low_row, high_row = dt[v, p], dt[v, NI - 3 + p]
            for j in range(p, 3):
                low_row = low_row + SCALE * SIXTIETHS[2 - j + p] * fh[0, v, j]
            for j in range(p + 1):
                high_row = high_row - SCALE * SIXTIETHS[2 - p + j] * fh[1, v, j]
            div[pl.ds(v * NI + p, S, stride=V * NI), :] = low_row
            div[pl.ds(v * NI + NI - 3 + p, S, stride=V * NI), :] = high_row
    start_deep(1, end_plane(1))
    gram = unpack(end_deep(0)) / count
    low = inverse_factor(gram)

    twice = low + pltpu.roll(low, S, axis=1)
    high = twice.astype(BF16)
    lhs = jnp.concatenate([high, (twice - high.astype(F32)).astype(BF16)], axis=0)[:, 0 : 2 * S]

    def mode_step(v, carry):
        for i in range(NI // 2):
            out = jnp.dot(lhs, yp[v, i], preferred_element_type=F32)
            out = out[0:S] + out[S : 2 * S]
            for r in range(2):
                modes[pl.ds(v * NI + 2 * i + r, S, stride=V * NI), :] = out[:, r * NL : (r + 1) * NL]
        return carry

    lax.fori_loop(0, V, mode_step, 0)
    cross = unpack(end_deep(1))
    root = jnp.sqrt(jnp.full((S, S), count, F32))
    red[...] = jnp.dot(low[:, 0:S], cross[:, 0:S], preferred_element_type=F32, precision=HIGHEST) / root


def write_kernel(modes, div, red, modes_out, div_out, red_out, sem):
    pairs = ((modes, modes_out), (div, div_out), (red, red_out))
    copies = [pltpu.make_async_copy(a, b, sem.at[i]) for i, (a, b) in enumerate(pairs)]
    for copy in copies:
        copy.start()
    for copy in copies:
        copy.wait()


def per_device(dims, snapshots):
    nz, nx, ny = dims
    count = float(V * NI * nz * nx * NL * ny * 2)
    vmem = pl.BlockSpec(memory_space=pltpu.VMEM)
    hbm = pl.BlockSpec(memory_space=pl.ANY)
    big = (S * V * NI, NL)
    dma = pltpu.SemaphoreType.DMA
    modes, div, red = pl.pallas_call(
        functools.partial(main_kernel, dims, count),
        out_shape=[pltpu.VMEM(big, F32), pltpu.VMEM(big, F32), pltpu.VMEM((S, S), F32)],
        in_specs=[hbm],
        out_specs=[vmem, vmem, vmem],
        scratch_shapes=[
            pltpu.VMEM((V, NI, S, NL), F32),
            pltpu.VMEM((V, NI // 2, 2 * S, 2 * NL), BF16),
            pltpu.VMEM((V, NI, S, NL), F32),
            pltpu.VMEM((2, V, 3, S, NL), F32),
            pltpu.VMEM((V, NI, S, NL), F32),
            pltpu.VMEM((V, NI, S, 2 * NL), BF16),
            pltpu.VMEM((4, NL, NL), BF16),
            pltpu.VMEM((4, 8 * V, NL), F32),
            pltpu.VMEM((V, 4, 8, NL), F32),
            pltpu.VMEM((2, V, 3, S, NL), F32),
            pltpu.VMEM((2, V, 4, 8, NL), F32),
            pltpu.VMEM((2 * S, NL), F32),
            pltpu.VMEM((6, 8, NL), F32),
            pltpu.VMEM((2, 8, NL), F32),
            pltpu.VMEM((2, nx * ny, 8, NL), F32),
            pltpu.VMEM((2, nz, 8, NL), F32),
            pltpu.SemaphoreType.REGULAR((2,)),
            dma,
            dma((10,)),
            dma((10,)),
        ],
        compiler_params=pltpu.CompilerParams(collective_id=0, has_side_effects=True),
    )(snapshots)
    pinned = [pltpu.with_memory_space_constraint(a, pltpu.VMEM) for a in (modes, div, red)]
    modes, div, red = pl.pallas_call(
        write_kernel,
        out_shape=[jax.ShapeDtypeStruct(big, F32), jax.ShapeDtypeStruct(big, F32), jax.ShapeDtypeStruct((S, S), F32)],
        in_specs=[vmem, vmem, vmem],
        out_specs=[hbm, hbm, hbm],
        scratch_shapes=[dma((3,))],
    )(*pinned)
    return modes.reshape(snapshots.shape), div.reshape(snapshots.shape), red


def solution(mesh):
    space, radial = mesh.shape["space"], mesh.shape["radial"]
    nx = 4 if space > 4 else 2
    placed = P(None, None, "space", "radial")
    return jax.shard_map(
        functools.partial(per_device, (space // nx, nx, radial // 2)),
        mesh=mesh,
        in_specs=(placed,),
        out_specs=(placed, placed, P()),
        check_vma=False,
    )
```

```python
import functools

import jax
import jax.numpy as jnp
from jax import lax
from jax.experimental import pallas as pl
from jax.experimental.pallas import tpu as pltpu
from jax.sharding import PartitionSpec as P

MESH = pl.DeviceIdType.MESH
F32 = jnp.float32
BF16 = jnp.bfloat16
HIGHEST = lax.Precision.HIGHEST
SIXTIETHS = (45.0, -9.0, 1.0)
SCALE = 1.0 / 60.0
S, V, NI, NL = 32, 5, 16, 128
NT = (((1,), (1,)), ((), ()))
TN = (((0,), (0,)), ((), ()))


def split(a):
    high = a.astype(BF16)
    low = (a - high.astype(F32)).astype(BF16)
    return jnp.concatenate([high, low], axis=0)


def parts(a):
    high = a.astype(BF16).astype(F32)
    return high, a - high


def flux_state(q):
    rho, ma, mb, mc, energy = q
    inv = 1.0 / rho
    ua, ub, uc = ma * inv, mb * inv, mc * inv
    press = 0.4 * (energy - 0.5 * (ma * ua + mb * ub + mc * uc))
    return ua, ub, press


def flux_axial(q):
    _, ma, mb, mc, energy = q
    ua, _, press = flux_state(q)
    return (ma, ma * ua + press, mb * ua, mc * ua, (energy + press) * ua)


def flux_radial(q):
    _, ma, mb, mc, energy = q
    _, ub, press = flux_state(q)
    return (mb, ma * ub, mb * ub + press, mc * ub, (energy + press) * ub)


def flux_both(q):
    _, ma, mb, mc, energy = q
    ua, ub, press = flux_state(q)
    cross, total = mb * ua, energy + press
    axial = (ma, ma * ua + press, cross, mc * ua, total * ua)
    radial = (mb, cross, mb * ub + press, mc * ub, total * ub)
    return axial, radial


def pack(acc, tmp, more=None):
    tmp[...] = jnp.zeros_like(tmp)
    tmp[:, 0:64] = acc
    full = tmp[...]
    rows = full[0:32] + full[32:64]
    both = rows + pltpu.roll(rows, NL - 32, axis=1)
    if more is not None:
        both = both + more[0:S]
        for r in (1, 2, 3):
            both = both + pltpu.roll(more[S * r : S * (r + 1)], NL - S * r, axis=1)
        both = both * SCALE
    lane = lax.broadcasted_iota(jnp.int32, (8, NL), 1)
    out = jnp.zeros((8, NL), F32)
    for r in range(4):
        part = both[8 * r : 8 * r + 8]
        if r:
            part = pltpu.roll(part, 32 * r, axis=1)
        out = jnp.where(lane // 32 == r, part, out)
    return out


def unpack(tile):
    return jnp.concatenate([tile] + [pltpu.roll(tile, NL - 32 * r, axis=1) for r in (1, 2, 3)], axis=0)


def inverse_factor(gram):
    row = lax.broadcasted_iota(jnp.int32, (S, NL), 0)
    lane = lax.broadcasted_iota(jnp.int32, (S, NL), 1)
    w = jnp.where(lane < S, gram, jnp.where(lane == row + S, 1.0, 0.0))
    for k in range(S - 1):
        pivot = w[k : k + 1, :]
        scale = w[:, k : k + 1] * (1.0 / w[k : k + 1, k : k + 1])
        w = w - jnp.where(row > k, scale, 0.0) * pivot
    diag = jnp.sum(jnp.where(lane == row, w, 0.0), axis=1, keepdims=True)
    low = pltpu.roll(w, NL - S, axis=1) * lax.rsqrt(diag)
    return jnp.where(lane < S, low, 0.0)


def offsets(n, steps):
    return sorted({d % n for k in steps for d in (k, -k)} - {0})


def main_kernel(dims, count, snap, modes, div, red, y, yp, fs, fh, dt, gs, gt, gz, ed, ha, hr, tmp, sb, rc, rp, rz, known, load_sem, send, recv):
    nz, nx, ny = dims
    nsp, nra = nz * nx, ny * 2
    sp, ra = lax.axis_index("space"), lax.axis_index("radial")
    z, x = sp // nx, sp % nx
    yy, c = ra // 2, ra % 2
    def plane(o):
        return (z * nx + (x + o[0]) % nx, ((yy + o[1]) % ny) * 2 + c)

    def deep(d):
        return (((z + d) % nz) * nx + x, ra)

    def nth_plane(n):
        half_x, half_y = nx // 2, ny // 2
        own = (nx - half_x) % nx * ny + (ny - half_y) % ny
        n = jnp.where(n >= own, n + 1, n)
        return plane((half_x + n // ny, half_y + n % ny))

    def nth_deep(n):
        return deep(nz // 2 + jnp.where(n % 2 == 1, nz - (n + 1) // 2, n // 2))

    core = (sp, yy * 2 + 1 - c)
    ahead_a, behind_a = ((sp + 1) % nsp, ra), ((sp + nsp - 1) % nsp, ra)
    ahead_r, behind_r = (sp, (ra + 1) % nra), (sp, (ra + nra - 1) % nra)

    barrier = pltpu.get_barrier_semaphore()
    line_x, line_y = [plane((d, 0)) for d in range(1, nx)], [plane((0, d)) for d in range(1, ny)]
    near_z, skip_z, far_z = [[deep(d) for d in offsets(nz, n)] for n in ((1, 2), (2,), (4,))]

    def signal(semaphore, targets):
        for peer in targets:
            pl.semaphore_signal(semaphore, inc=1, device_id=peer, device_id_type=MESH)
        return len(targets)

    near = signal(barrier, [ahead_a, behind_a, ahead_r, behind_r, core] + near_z + line_x + line_y)
    for v in range(V):
        for s in range(S):
            pltpu.make_async_copy(snap.at[s, v], y.at[v, :, s, :], load_sem.at[v]).start()

    def loaded(v):
        pltpu.make_async_copy(y.at[v], y.at[v], load_sem.at[v]).wait()

    def remote(src, dst, k, peer):
        return pltpu.make_async_remote_copy(src, dst, send.at[k], recv.at[k], device_id=peer, device_id_type=MESH)

    row8 = lax.broadcasted_iota(jnp.int32, (8, NL), 0)
    lane8 = lax.broadcasted_iota(jnp.int32, (8, NL), 1)
    row16 = lax.broadcasted_iota(jnp.int32, (16, 2 * NL), 0)
    lane16 = lax.broadcasted_iota(jnp.int32, (16, 2 * NL), 1)
    cell = row16 % 8
    pick = (cell < 6) & (lane16 == row16 // 8 * NL + jnp.where(cell < 3, cell, cell + NL - 6))
    pick = jnp.where(pick, 1.0, 0.0).astype(BF16)

    def gram_step(v, acc):
        for j in range(4):
            edge = []
            for i in (2 * j, 2 * j + 1):
                p = split(jnp.concatenate([y[v, 2 * i], y[v, 2 * i + 1]], axis=1))
                yp[v, i] = p
                out = lax.dot_general(jnp.concatenate([p, pick], axis=0), p, NT, preferred_element_type=F32)
                acc = acc + out[0 : 2 * S]
                for r in (2 * S, 2 * S + 8):
                    edge.append(out[r : r + 8, 0:S] + out[r : r + 8, S : 2 * S])
            ed[v, j] = jnp.concatenate(edge, axis=1)
        return acc

    acc = jnp.zeros((2 * S, 2 * S), F32)
    for v in range(2):
        loaded(v)
        acc = gram_step(v, acc)
    for v in range(2, V):
        loaded(v)
    pl.semaphore_wait(barrier, near)

    first_halo = remote(y.at[:, pl.ds((1 - c) * (NI - 3), 3)], ha.at[c], 0, ((sp + nsp + 1 - 2 * c) % nsp, ra))
    other_halo = remote(y.at[:, pl.ds(c * (NI - 3), 3)], ha.at[1 - c], 1, ((sp + nsp - 1 + 2 * c) % nsp, ra))
    has_behind, has_ahead = jnp.where(sp > 0, 1, 0), jnp.where(sp < nsp - 1, 1, 0)
    first_sent = jnp.where(c == 0, has_ahead, has_behind) > 0
    first_due = jnp.where(c == 0, has_behind, has_ahead) > 0

    @pl.when(first_sent)
    def _():
        first_halo.start()

    @pl.when(first_due)
    def _():
        other_halo.start()

    near = signal(known.at[0], line_x + skip_z)

    def start_core(k, tile):
        sb[3 * k] = tile
        remote(sb.at[3 * k], rc.at[k], 4 + 3 * k, core).start()

    def end_core(k):
        remote(sb.at[3 * k], rc.at[k], 4 + 3 * k, core).wait()
        return sb[3 * k] + rc[k]

    def start_many(k, stage, buf, mine, n, target, tile):
        sb[3 * k + stage] = tile
        buf[k, mine] = tile

        def send_one(i, carry):
            remote(sb.at[3 * k + stage], buf.at[k, mine], 4 + 3 * k + stage, target(i)).start()
            return carry

        lax.fori_loop(0, n - 1, send_one, 0)

    def end_many(k, stage, buf, n):
        landed = buf.at[k, 0 : n - 1]
        pltpu.make_async_copy(landed, landed, recv.at[4 + 3 * k + stage]).wait()
        pltpu.make_async_copy(landed, landed, send.at[4 + 3 * k + stage]).wait()
        terms = [buf[k, i] for i in range(n)]
        while len(terms) > 1:
            terms = [terms[i] + terms[i + 1] for i in range(0, len(terms), 2)]
        return terms[0]

    def start_plane(k, tile):
        start_many(k, 1, rp, x * ny + yy, nx * ny, nth_plane, tile)

    def end_plane(k):
        return end_many(k, 1, rp, nx * ny)

    def start_deep(k, tile):
        start_many(k, 2, rz, z, nz, nth_deep, tile)

    def end_deep(k):
        return end_many(k, 2, rz, nz)

    acc = lax.fori_loop(2, V, gram_step, acc)
    start_core(0, pack(acc, tmp))
    radial_halo = [remote(ed, hr.at[0], 2, ahead_r), remote(ed, hr.at[1], 3, behind_r)]
    for h in radial_halo:
        h.start()


    def flux_step(i, carry):
        axial, radial = flux_both([y[v, i] for v in range(V)])
        for v in range(V):
            fs[v, i] = axial[v]
            high = radial[v].astype(BF16)
            gs[v, i, :, 0:NL] = high
            gs[v, i, :, NL : 2 * NL] = (radial[v] - high.astype(F32)).astype(BF16)
        return carry

    lax.fori_loop(0, NI, flux_step, 0)
    tile = end_core(0)
    pl.semaphore_wait(known.at[0], near)
    start_plane(0, tile)
    far = signal(known.at[1], far_z)
    shift = lax.broadcasted_iota(jnp.int32, (NL, NL), 1) - lax.broadcasted_iota(jnp.int32, (NL, NL), 0)
    matrix = jnp.zeros((NL, NL), F32)
    for k, cf in zip((1, 2, 3), SIXTIETHS):
        matrix = jnp.where(shift == k, cf, jnp.where(shift == -k, -cf, matrix))
    matrix = jnp.concatenate([matrix, matrix], axis=0).astype(BF16)

    def radial_step(v, carry):
        out = jnp.dot(gs[v].reshape(NI * S, 2 * NL), matrix, preferred_element_type=F32)
        dt[v] = out.reshape(NI, S, NL)
        return carry

    lax.fori_loop(0, V, radial_step, 0)

    def axial_step(v, acc):
        for i in range(NI // 2):
            pair = []
            for r in (2 * i, 2 * i + 1):
                total = dt[v, r]
                for k, cf in zip((1, 2, 3), SIXTIETHS):
                    if k <= r < NI - k:
                        total = total + cf * (fs[v, r - k] - fs[v, r + k])
                    else:
                        total = total + cf * fs[v, r - k] if r >= k else total - cf * fs[v, r + k]
                dt[v, r] = total
                pair.append(total)
            acc = acc + lax.dot_general(yp[v, i], split(jnp.concatenate(pair, axis=1)), NT, preferred_element_type=F32)
        return acc

    acc = lax.fori_loop(0, V, axial_step, jnp.zeros((2 * S, 2 * S), F32))

    def halo_flux(side):
        keep = jnp.full((S, NL), jnp.where(side == 0, jnp.where(sp > 0, 1, 0), jnp.where(sp < nsp - 1, 1, 0))) > 0
        for j in range(3):
            axial = flux_axial([ha[side, v, j] for v in range(V)])
            for v in range(V):
                fh[side, v, j] = jnp.where(keep, axial[v], 0.0)
        return keep

    lower = jnp.where(c == 0, 1.0, 0.0)

    def cross_coeff(mine, theirs):
        if mine == theirs:
            return SIXTIETHS[2]
        if mine < theirs:
            return SIXTIETHS[2 - theirs + mine] * lower
        return SIXTIETHS[2 - mine + theirs] * (1.0 - lower)

    def land(copy, due, side):
        @pl.when(due)
        def _():
            copy.wait_recv()

        @pl.when(jnp.logical_not(due))
        def _():
            ha[side] = jnp.ones((V, 3, S, NL), F32)

    land(first_halo, first_due, c)
    keep = halo_flux(c)
    sign = 2.0 * lower - 1.0

    def cross_step(v, acc):
        theirs = [fh[c, v, j] for j in range(3)]
        mine = [fs[v, c * (NI - 3) + j] for j in range(3)]
        for p in range(3):
            near_mine = sign * sum(cross_coeff(p, j) * theirs[j] for j in range(3))
            near_theirs = -sign * sum(cross_coeff(j, p) * mine[j] for j in range(3))
            left = jnp.concatenate([y[v, c * (NI - 3) + p], jnp.where(keep, ha[c, v, p], 0.0)], axis=1)
            right = jnp.concatenate([near_mine, near_theirs], axis=1)
            acc = acc + lax.dot_general(split(left), split(right), NT, preferred_element_type=F32)
        return acc

    acc = lax.fori_loop(0, V, cross_step, acc)

    for h in radial_halo:
        h.wait()
    edge = lax.broadcasted_iota(jnp.int32, (8 * V, 8 * V), 0)
    ghost = lax.broadcasted_iota(jnp.int32, (8 * V, 8 * V), 1)
    same, edge, ghost = edge // 8 == ghost // 8, edge % 8, ghost % 8
    high_side = jnp.where((ghost < 3) & (edge >= 3) & (edge < 6), 6 + ghost - edge, 0)
    low_side = jnp.where((ghost >= 3) & (ghost < 6) & (edge < 3), 6 + edge - ghost, 0)
    link = jnp.zeros((8 * V, 8 * V), F32)
    for k, cf in zip((1, 2, 3), SIXTIETHS):
        link = jnp.where(same & (low_side == k), cf, jnp.where(same & (high_side == k), -cf, link))
    valid = jnp.where(row8 < 3, jnp.where(ra < nra - 1, 1, 0), jnp.where((row8 < 6) & (ra > 0), 1, 0)) > 0
    blank = jnp.zeros((8, NL), F32)
    more = jnp.zeros((NL, NL), F32)
    for j in range(4):
        cells = [jnp.where(row8 < 3, hr[1, v, j], hr[0, v, j]) for v in range(V)]
        cells[0] = jnp.where(row8 < 6, cells[0], 1.0)
        ghosts = jnp.concatenate([jnp.where(valid, g, 0.0) for g in flux_radial(cells)], axis=0)
        gz[j] = ghosts
        added = parts(jnp.dot(link, ghosts, preferred_element_type=F32, precision=HIGHEST))
        mine = parts(jnp.concatenate([ed[v, j] for v in range(V)], axis=0))
        left = jnp.concatenate([a for m in (0, 1, 0, 1) for a in (mine[m], blank)], axis=0)
        right = jnp.concatenate([a for m in (0, 0, 1, 1) for a in (added[m], blank)], axis=0)
        more = more + lax.dot_general(left.astype(BF16), right.astype(BF16), TN, preferred_element_type=F32)
    start_core(1, pack(acc, tmp, more))

    tile = end_plane(0)
    if far:
        pl.semaphore_wait(known.at[1], far)
    start_deep(0, tile)
    start_plane(1, end_core(1))

    step = jnp.where(row8 < 3, row8 + NL - lane8, lane8 + 6 - row8)
    weight = jnp.zeros((8, NL), F32)
    for k, cf in zip((1, 2, 3), SIXTIETHS):
        weight = jnp.where(step == k, cf, weight)
    weight = jnp.where(row8 < 6, jnp.where(row8 < 3, -weight, weight), 0.0)
    weights = jnp.concatenate([weight] * 16, axis=0)
    group = (lax.broadcasted_iota(jnp.int32, (NL, NL), 0) // 8) % 8
    blank = jnp.zeros((24, NL), F32)
    for j in range(4):
        high, low = parts(gz[j])
        gt[j] = jnp.concatenate([high, blank, low, blank], axis=0).T.astype(BF16)
    for v in range(V):
        out = jnp.dot(gt[...].reshape(NI * S, NL), jnp.where(group == v, weights, 0.0).astype(BF16), preferred_element_type=F32)
        dt[v] = (dt[v] + out.reshape(NI, S, NL)) * SCALE
        for i in range(3, NI - 3):
            div[pl.ds(v * NI + i, S, stride=V * NI), :] = dt[v, i]

    land(other_halo, first_sent, 1 - c)
    halo_flux(1 - c)

    @pl.when(first_sent)
    def _():
        first_halo.wait_send()

    @pl.when(first_due)
    def _():
        other_halo.wait_send()

    for v in range(V):
        for p in range(3):
            low_row, high_row = dt[v, p], dt[v, NI - 3 + p]
            for j in range(p, 3):
                low_row = low_row + SCALE * SIXTIETHS[2 - j + p] * fh[0, v, j]
            for j in range(p + 1):
                high_row = high_row - SCALE * SIXTIETHS[2 - p + j] * fh[1, v, j]
            div[pl.ds(v * NI + p, S, stride=V * NI), :] = low_row
            div[pl.ds(v * NI + NI - 3 + p, S, stride=V * NI), :] = high_row
    start_deep(1, end_plane(1))
    gram = unpack(end_deep(0)) / count
    low = inverse_factor(gram)

    twice = low + pltpu.roll(low, S, axis=1)
    high = twice.astype(BF16)
    lhs = jnp.concatenate([high, (twice - high.astype(F32)).astype(BF16)], axis=0)[:, 0 : 2 * S]

    def mode_step(v, carry):
        for i in range(NI // 2):
            out = jnp.dot(lhs, yp[v, i], preferred_element_type=F32)
            out = out[0:S] + out[S : 2 * S]
            for r in range(2):
                modes[pl.ds(v * NI + 2 * i + r, S, stride=V * NI), :] = out[:, r * NL : (r + 1) * NL]
        return carry

    lax.fori_loop(0, V, mode_step, 0)
    cross = unpack(end_deep(1))
    root = jnp.sqrt(jnp.full((S, S), count, F32))
    red[...] = jnp.dot(low[:, 0:S], cross[:, 0:S], preferred_element_type=F32, precision=HIGHEST) / root


def write_kernel(modes, div, red, modes_out, div_out, red_out, sem):
    pairs = ((modes, modes_out), (div, div_out), (red, red_out))
    copies = [pltpu.make_async_copy(a, b, sem.at[i]) for i, (a, b) in enumerate(pairs)]
    for copy in copies:
        copy.start()
    for copy in copies:
        copy.wait()


def per_device(dims, snapshots):
    nz, nx, ny = dims
    count = float(V * NI * nz * nx * NL * ny * 2)
    vmem = pl.BlockSpec(memory_space=pltpu.VMEM)
    hbm = pl.BlockSpec(memory_space=pl.ANY)
    big = (S * V * NI, NL)
    dma = pltpu.SemaphoreType.DMA
    modes, div, red = pl.pallas_call(
        functools.partial(main_kernel, dims, count),
        out_shape=[pltpu.VMEM(big, F32), pltpu.VMEM(big, F32), pltpu.VMEM((S, S), F32)],
        in_specs=[hbm],
        out_specs=[vmem, vmem, vmem],
        scratch_shapes=[
            pltpu.VMEM((V, NI, S, NL), F32),
            pltpu.VMEM((V, NI // 2, 2 * S, 2 * NL), BF16),
            pltpu.VMEM((V, NI, S, NL), F32),
            pltpu.VMEM((2, V, 3, S, NL), F32),
            pltpu.VMEM((V, NI, S, NL), F32),
            pltpu.VMEM((V, NI, S, 2 * NL), BF16),
            pltpu.VMEM((4, NL, NL), BF16),
            pltpu.VMEM((4, 8 * V, NL), F32),
            pltpu.VMEM((V, 4, 8, NL), F32),
            pltpu.VMEM((2, V, 3, S, NL), F32),
            pltpu.VMEM((2, V, 4, 8, NL), F32),
            pltpu.VMEM((2 * S, NL), F32),
            pltpu.VMEM((6, 8, NL), F32),
            pltpu.VMEM((2, 8, NL), F32),
            pltpu.VMEM((2, nx * ny, 8, NL), F32),
            pltpu.VMEM((2, nz, 8, NL), F32),
            pltpu.SemaphoreType.REGULAR((2,)),
            dma((V,)),
            dma((10,)),
            dma((10,)),
        ],
        compiler_params=pltpu.CompilerParams(collective_id=0, has_side_effects=True),
    )(snapshots)
    pinned = [pltpu.with_memory_space_constraint(a, pltpu.VMEM) for a in (modes, div, red)]
    modes, div, red = pl.pallas_call(
        write_kernel,
        out_shape=[jax.ShapeDtypeStruct(big, F32), jax.ShapeDtypeStruct(big, F32), jax.ShapeDtypeStruct((S, S), F32)],
        in_specs=[vmem, vmem, vmem],
        out_specs=[hbm, hbm, hbm],
        scratch_shapes=[dma((3,))],
    )(*pinned)
    return modes.reshape(snapshots.shape), div.reshape(snapshots.shape), red


def solution(mesh):
    space, radial = mesh.shape["space"], mesh.shape["radial"]
    nx = 4 if space > 4 else 2
    placed = P(None, None, "space", "radial")
    return jax.shard_map(
        functools.partial(per_device, (space // nx, nx, radial // 2)),
        mesh=mesh,
        in_specs=(placed,),
        out_specs=(placed, placed, P()),
        check_vma=False,
    )
```
